32 devices in a mesh: parts: 2 (over y), mesh: 4 (over z), tile: 2 (over x), feat: 2 (over core).
Axes of the slice: x: 2, y: 2, z: 4, core: 2. Of those that a mesh axis runs over, the one named last changes fastest.
Arguments:
- fields: bfloat16 [2048, 128], P(('parts', 'mesh', 'tile')), parts along dimension 0, may hold values from -6 to 6
- owner_group: int32 [1024, 1], P(('mesh', 'tile')), may hold values from 0 to 7; in each aligned block of 128 rows (0 to 127, 128 to 255, ...) at most 32 rows name the same one
- owner_node: int32 [1024], P(('mesh', 'tile')), may hold values from 0 to 31
- stencil_codes: int32 [256, 8], P(('mesh', 'tile')), may hold values from 0 to 24
- coarse_ids: int32 [256], P(('mesh', 'tile')), may hold values from 0 to 15
- encode_weight: bfloat16 [128, 512], P(None, 'feat'), may hold values from -0.5 to 0.5
- process_weight: bfloat16 [512, 512], P(None, 'feat'), may hold values from -0.09375 to 0.09375
- coarse_weight: bfloat16 [512, 512], P(None, 'feat'), may hold values from -0.0625 to 0.0625
- decode_weight: bfloat16 [512, 128], P('feat'), may hold values from -0.25 to 0.25
- cotangent: float32 [2048, 128], P(('parts', 'mesh', 'tile')), parts along dimension 0, may hold values from -6 to 6
Outputs:
- prediction: float32 [2048, 128], P(('parts', 'mesh', 'tile')), parts along dimension 0
- encode_grad: float32 [256, 512], P('parts', 'feat'), parts along dimension 0
- process_grad: float32 [1024, 512], P('parts', 'feat'), parts along dimension 0
- coarse_grad: float32 [1024, 512], P('parts', 'feat'), parts along dimension 0
- decode_grad: float32 [1024, 128], P(('parts', 'feat')), parts along dimension 0
The draws below stay inside these ranges and needn't reach their ends.
There are 2 independent parts, one for each index of `parts`. The reference program is written for one: setup_inputs(seed, part) draws one part's arguments, and reference() takes and returns one part's arrays. A program takes and returns all parts, laid end to end along the dimension named above; an argument that names none is the same for every part. Nothing has to cross between parts.
Inputs may be any that keep to these rules, and one draw needn't show every extreme that they name: `owner_group`: in the rows of one device group no value is named more than 32 times.
All inputs are finite; a program needn't handle non-finite values.
Results may differ from the reference program's by a relative error of at most 0.0073.
Values may be sent and summed in bfloat16 or wider, within the bound.
A program may use at most 64 MiB of HBM per device.

```python
import math
import jax
import jax.numpy as jnp
import numpy as np
from jax import lax

H = 512
C_IN = 128
C_OUT = 128
GB = 128
MA = 4
MB = 8
K = 8
CPD = 2
CAP = 32
GRID = 1024
NODES = 256
NC = 16
N_MESH = 4
N_TILE = 2


def draw_coarse_ids(key, part):
    key_near, key_far, key_pick = jax.random.split(jax.random.fold_in(key, 17), 3)
    owner_block = jnp.arange(NODES, dtype=jnp.int32) // (MA * MB)
    nearby = (owner_block * CPD + jax.random.randint(key_near, (NODES,), 0, 2 * CPD)) % NC
    anywhere = jax.random.randint(key_far, (NODES,), 0, NC)
    choose = jax.random.randint(key_pick, (NODES,), 0, 2)
    return jnp.where(choose == 0, nearby, anywhere).astype(jnp.int32)


def touch_ends(result, key, smallest, high):
    place = [jax.random.randint(jax.random.fold_in(key, axis), (), 0, length) for axis, length in enumerate(result.shape)]
    main_axis = result.shape.index(max(result.shape))
    beside = place[:main_axis] + [(place[main_axis] + 1) % result.shape[main_axis]] + place[main_axis + 1:]
    return result.at[tuple(place)].set(smallest).at[tuple(beside)].set(high)


def steps_of(key, extent, cuts, least, high):
    gain, own = 1.0, jax.random.fold_in(key, 6)
    for position, shards_of in cuts:
        steps = jnp.exp(jax.random.uniform(jax.random.fold_in(own, position), (shards_of,), jnp.float32, least / len(cuts), high / len(cuts)))
        gain = gain * jnp.repeat(steps, extent[position] // shards_of).reshape([-1 if axis == position else 1 for axis in range(len(extent))])
    return gain


def shared_out(stream_key, own, number, rows, count, top, bound, slope):
    ranking = jax.random.permutation(stream_key, count)
    packed, common = shares(count, rows * top, bound, slope, True), shares(count, rows * top, bound, slope, False)
    places = jnp.arange(count)

    def named(tallies, offset_by):
        used = int((tallies > 0).sum())
        fixed = max(1, used // 4)
        passed = fixed + (places - fixed + offset_by * (used - fixed)) % max(1, count - fixed)
        return jnp.zeros((count,), jnp.int32).at[ranking[jnp.where(places < fixed, places, passed)]].set(jnp.asarray(tallies, jnp.int32))

    tallies = jnp.where(number % 4 == 0, named(packed, number // 4), named(common, number - number // 4 - 1))
    mixed = jax.random.permutation(jax.random.fold_in(own, 3), count)
    giver, sink = mixed[0:count // 2 * 2:2], mixed[1:count // 2 * 2:2]
    margin = jnp.minimum(tallies[giver] - 1, bound - tallies[sink]) // 2
    margin = jnp.where((giver == ranking[0]) | (sink == ranking[0]) | (tallies[sink] == 0), 0, jnp.maximum(margin, 0))
    passed = jax.random.randint(jax.random.fold_in(own, 4), (count // 2,), 0, 1 << 20) % (margin + 1)
    tallies = tallies.at[giver].add(-passed).at[sink].add(passed)
    members = jnp.searchsorted(jnp.cumsum(tallies), jnp.arange(rows * top), side="right").astype(jnp.int32)
    grid = members.reshape(top, rows).T
    grid = grid[jax.random.permutation(jax.random.fold_in(own, 1), rows)]
    offset_by = jax.random.randint(jax.random.fold_in(own, 2), (rows, 1), 0, top)
    return jnp.take_along_axis(grid, (jnp.arange(top)[None, :] + offset_by) % top, axis=1)


def shares(count, total, reach, skew, full):
    loads = [(1 << 20) // math.isqrt(standing ** skew) + 1 for standing in range(1, count + 1)]
    largest = reach if full else min(reach, max(-(-total // count), total * loads[0] // sum(loads)))
    least = 1 if total - largest >= count - 1 else 0
    given, spare = [largest] + [least] * (count - 1), total - largest - least * (count - 1)
    while spare > 0:
        movable = [i for i in range(1, count) if given[i] < largest] or [i for i in range(1, count) if given[i] < reach]
        whole, left = sum([loads[i] for i in movable]), spare
        for i in movable:
            more = min(reach - given[i], max(1, left * loads[i] // whole), spare)
            given[i] = given[i] + more
            spare = spare - more
    return np.array(given)


def centred(key, dims, scale, bound, cuts=(), kind=jnp.bfloat16):
    drawn = jax.random.normal(key, dims, jnp.float32) * scale
    if len(cuts) > 0:
        drawn = steps_of(key, dims, cuts, -0.22, 0.18) * drawn
    return jnp.clip(drawn, min=-bound, max=bound).astype(kind)


def setup_inputs(seed: int = 0, part: int = 0) -> dict:
    key_of = jax.random.split(jax.random.key(seed), 11)
    part_splits = jax.random.split(jax.random.fold_in(key_of[10], part), 11)
    fields = centred(part_splits[0], (GRID, C_IN), 1.0, 6.0, ((0, 8),))
    owner_group_keys = jax.random.split(jax.random.fold_in(key_of[1], 1), GRID // GB)
    owner_group_turns = jax.random.permutation(jax.random.fold_in(key_of[1], 3), GRID // GB)
    owner_group = jax.vmap(lambda own, number: shared_out(jax.random.fold_in(key_of[1], 2), own, number, GB, N_MESH * N_TILE, 1, CAP, 2))(owner_group_keys, owner_group_turns).reshape((GRID, 1))
    owner_node = touch_ends(jax.random.randint(key_of[2], (GRID,), 0, MA * MB), jax.random.fold_in(key_of[2], 1), 0, (MA * MB) - 1).astype(jnp.int32)
    stencil_codes = touch_ends(jax.random.randint(key_of[3], (NODES, K), 0, 25), jax.random.fold_in(key_of[3], 1), 0, 24).astype(jnp.int32)
    coarse_ids = draw_coarse_ids(jax.random.fold_in(key_of[10], 71), part)
    encode_weight = centred(key_of[5], (C_IN, H), C_IN ** -0.5, 0.5, ((1, 2),))
    process_weight = centred(key_of[6], (H, H), (H * K) ** -0.5, 0.09375, ((1, 2),))
    coarse_weight = centred(key_of[7], (H, H), (H * MA * MB // CPD) ** -0.5, 0.0625, ((1, 2),))
    decode_weight = centred(key_of[8], (H, C_OUT), H ** -0.5, 0.25, ((0, 2),))
    cotangent = centred(part_splits[9], (GRID, C_OUT), 1.0, 6.0, ((0, 8),), jnp.float32)
    return {"fields": fields, "owner_group": owner_group, "owner_node": owner_node, "stencil_codes": stencil_codes, "coarse_ids": coarse_ids, "encode_weight": encode_weight, "process_weight": process_weight, "coarse_weight": coarse_weight, "decode_weight": decode_weight, "cotangent": cotangent}


def silu_grad(pre):
    sig = jax.nn.sigmoid(pre)
    return sig * (1.0 + pre * (1.0 - sig))

def to_torus(values):
    width_last = values.shape[-1]
    shaped = values.reshape(N_MESH, N_TILE, MA, MB, width_last)
    return jnp.transpose(shaped, (0, 2, 1, 3, 4)).reshape(N_MESH * MA, N_TILE * MB, width_last)

def from_torus(values):
    width_last = values.shape[-1]
    shaped = values.reshape(N_MESH, MA, N_TILE, MB, width_last)
    return jnp.transpose(shaped, (0, 2, 1, 3, 4)).reshape(NODES, width_last)

def reference(fields, owner_group, owner_node, stencil_codes, coarse_ids, encode_weight, process_weight, coarse_weight, decode_weight, cotangent):
    highest = lax.Precision.HIGHEST
    target = (owner_group[:, 0] * (MA * MB) + owner_node).astype(jnp.int32)
    pre_encode = jnp.dot(fields, encode_weight, preferred_element_type=jnp.float32)
    hidden = jax.nn.silu(pre_encode).astype(jnp.bfloat16)
    node_in = jax.ops.segment_sum(hidden.astype(jnp.float32), target, NODES).astype(jnp.bfloat16)
    counts = lax.optimization_barrier(jnp.sum((stencil_codes[:, :, None] == jnp.arange(25, dtype=jnp.int32)[None, None, :]).astype(jnp.float32), axis=1))
    count_grid = to_torus(counts)
    node_grid = to_torus(node_in.astype(jnp.float32))
    gathered = jnp.zeros(node_grid.shape, jnp.float32)
    for code_index in range(25):
        step_x = code_index // 5 - 2
        step_y = code_index % 5 - 2
        gathered = gathered + count_grid[:, :, code_index:code_index + 1] * jnp.roll(node_grid, (-step_x, -step_y), axis=(0, 1))
    agg = from_torus(gathered).astype(jnp.bfloat16)
    pre_mesh = jnp.dot(agg, process_weight, preferred_element_type=jnp.float32)
    level_one = node_in.astype(jnp.float32) + jax.nn.silu(pre_mesh)
    coarse_in = jax.ops.segment_sum(level_one, coarse_ids, NC).astype(jnp.bfloat16)
    pre_coarse = jnp.dot(coarse_in, coarse_weight, preferred_element_type=jnp.float32)
    coarse_out = jax.nn.silu(pre_coarse).astype(jnp.bfloat16)
    level_two = (level_one + coarse_out.astype(jnp.float32)[coarse_ids]).astype(jnp.bfloat16)
    merged = (hidden.astype(jnp.float32) + level_two.astype(jnp.float32)[target]).astype(jnp.bfloat16)
    prediction = jnp.dot(merged, decode_weight, preferred_element_type=jnp.float32)
    decode_grad = jnp.dot(merged.astype(jnp.float32).T, cotangent, precision=highest)
    grad_merged = jnp.dot(cotangent, decode_weight.astype(jnp.float32).T, precision=highest)
    grad_rows = grad_merged.astype(jnp.bfloat16)
    grad_two = jax.ops.segment_sum(grad_rows.astype(jnp.float32), target, NODES)
    grad_coarse_out = jax.ops.segment_sum(grad_two, coarse_ids, NC)
    grad_pre_coarse = grad_coarse_out * silu_grad(pre_coarse)
    coarse_grad = jnp.dot(coarse_in.astype(jnp.float32).T, grad_pre_coarse, precision=highest)
    grad_coarse_in = jnp.dot(grad_pre_coarse, coarse_weight.astype(jnp.float32).T, precision=highest)
    grad_one = grad_two + grad_coarse_in[coarse_ids]
    grad_pre_mesh = grad_one * silu_grad(pre_mesh)
    process_grad = jnp.dot(agg.astype(jnp.float32).T, grad_pre_mesh, precision=highest)
    grad_agg = jnp.dot(grad_pre_mesh, process_weight.astype(jnp.float32).T, precision=highest).astype(jnp.bfloat16)
    grad_grid = to_torus(grad_agg.astype(jnp.float32))
    spread = jnp.zeros(grad_grid.shape, jnp.float32)
    for code_index in range(25):
        step_x = code_index // 5 - 2
        step_y = code_index % 5 - 2
        spread = spread + jnp.roll(count_grid[:, :, code_index:code_index + 1] * grad_grid, (step_x, step_y), axis=(0, 1))
    grad_zero = (grad_one + from_torus(spread)).astype(jnp.bfloat16)
    grad_hidden = grad_merged + grad_zero.astype(jnp.float32)[target]
    grad_pre_encode = grad_hidden * silu_grad(pre_encode)
    encode_grad = jnp.dot(fields.astype(jnp.float32).T, grad_pre_encode, precision=highest)
    return (prediction, encode_grad, process_grad, coarse_grad, decode_grad)
```

```python
import functools

import jax
import jax.numpy as jnp
from jax import lax
from jax.experimental import pallas as pl
from jax.experimental.pallas import tpu as pltpu
from jax.sharding import PartitionSpec as P

MA = 4
MB = 8
CPD = 2


def padded(array, sides, width):
    for axis, dim in sides:
        peers, length = (lax.axis_size(axis), array.shape[dim])
        up = [(i, (i + 1) % peers) for i in range(peers)]
        down = [(j, i) for i, j in up]
        last = lax.slice_in_dim(array, length - width, length, axis=dim)
        initial = lax.slice_in_dim(array, 0, width, axis=dim)
        before = lax.ppermute(last, axis, up)
        after = lax.ppermute(initial, axis, down)
        array = jnp.concatenate([before, array, after], axis=dim)
    return array


def silu_grad(pre):
    sig = jax.nn.sigmoid(pre)
    return sig * (1.0 + pre * (1.0 - sig))


def send_rows(outgoing, slot_node):
    feat_width = outgoing.shape[-1]
    got, got_node = (
        lax.all_to_all(outgoing, ("mesh", "tile"), split_axis=0, concat_axis=0, tiled=True),
        lax.all_to_all(slot_node, ("mesh", "tile"), split_axis=0, concat_axis=0, tiled=True),
    )
    return (got.reshape(-1, feat_width), got_node.reshape(-1))


def route_block(block, mesh_count, tile_count, purpose):
    feat_width = block.shape[-1]
    slot_count = block.shape[0] // (mesh_count * tile_count)
    flat_shape = (mesh_count * tile_count, slot_count, feat_width)
    if purpose == "reply":
        moved = lax.all_to_all(
            block.reshape(flat_shape), ("mesh", "tile"), split_axis=0, concat_axis=0, tiled=True
        )
    elif purpose == "gradient":
        moved = lax.all_to_all(
            block.reshape(flat_shape), ("mesh", "tile"), split_axis=0, concat_axis=0, tiled=True
        )
    else:
        moved = lax.all_to_all(
            block.reshape(flat_shape), ("mesh", "tile"), split_axis=0, concat_axis=0, tiled=True
        )
    return moved.reshape(-1, feat_width)


def body(
    fields,
    owner_group,
    owner_node,
    stencil_codes,
    coarse_ids,
    encode_weight,
    process_weight,
    coarse_weight,
    decode_weight,
    cotangent,
):
    highest = lax.Precision.HIGHEST
    row_count = fields.shape[0]
    mesh_count = lax.axis_size("mesh")
    tile_count = lax.axis_size("tile")
    groups = mesh_count * tile_count
    slot_count = 2 * row_count // groups
    feat_width = encode_weight.shape[1]
    patch_rows = MA
    patch_cols = MB
    nodes_local = patch_rows * patch_cols
    coarse_count = CPD * groups
    target = owner_group[:, 0]
    group_onehot = (target[:, None] == jnp.arange(groups, dtype=jnp.int32)[None, :]).astype(
        jnp.int32
    )
    earlier = jnp.cumsum(group_onehot, axis=0) - group_onehot
    position = target * slot_count + jnp.sum(earlier * group_onehot, axis=1)
    matches = jnp.arange(groups * slot_count, dtype=jnp.int32)[:, None] == position[None, :]
    dispatch = matches.astype(jnp.bfloat16)
    slot_node = (jnp.max(jnp.where(matches, owner_node[None, :] + 1, 0), axis=1) - 1).reshape(
        groups, slot_count
    )
    pre_encode = jnp.dot(fields, encode_weight, preferred_element_type=jnp.float32)
    hidden = jax.nn.silu(pre_encode).astype(jnp.bfloat16)
    outgoing = jnp.dot(dispatch, hidden, preferred_element_type=jnp.float32).astype(jnp.bfloat16)
    incoming, incoming_node = send_rows(outgoing.reshape(groups, slot_count, feat_width), slot_node)
    node_match = (
        incoming_node[:, None] == jnp.arange(nodes_local, dtype=jnp.int32)[None, :]
    ).astype(jnp.bfloat16)
    node_in = jnp.einsum(
        "sn,sh->nh", node_match, incoming, preferred_element_type=jnp.float32
    ).astype(jnp.bfloat16)
    counts = jnp.sum(
        (stencil_codes[:, :, None] == jnp.arange(25, dtype=jnp.int32)[None, None, :]).astype(
            jnp.float32
        ),
        axis=1,
    )
    counts = counts.astype(jnp.bfloat16).reshape(patch_rows, patch_cols, 25)
    padded_nodes, padded_counts = (
        padded(node_in.reshape(patch_rows, patch_cols, feat_width), (("mesh", 0), ("tile", 1)), 2),
        padded(counts, (("mesh", 0), ("tile", 1)), 2),
    )
    gathered = jnp.zeros((patch_rows, patch_cols, feat_width), jnp.float32)
    for code_index in range(25):
        step_x = code_index // 5 - 2
        step_y = code_index % 5 - 2
        weight_here = padded_counts[
            2 : 2 + patch_rows, 2 : 2 + patch_cols, code_index : code_index + 1
        ].astype(jnp.float32)
        gathered = gathered + weight_here * padded_nodes[
            2 + step_x : 2 + step_x + patch_rows, 2 + step_y : 2 + step_y + patch_cols
        ].astype(jnp.float32)
    agg = gathered.reshape(nodes_local, feat_width).astype(jnp.bfloat16)
    agg_full = lax.all_gather(agg, "feat", axis=1, tiled=True)
    pre_mesh = jnp.dot(agg_full, process_weight, preferred_element_type=jnp.float32)
    level_one = node_in.astype(jnp.float32) + jax.nn.silu(pre_mesh)
    coarse_match = (
        coarse_ids[:, None] == jnp.arange(coarse_count, dtype=jnp.int32)[None, :]
    ).astype(jnp.float32)
    coarse_part = jnp.dot(coarse_match.T, level_one, precision=highest)
    coarse_total = lax.psum(coarse_part, ("mesh", "tile"))
    coarse_in = lax.all_gather(coarse_total.astype(jnp.bfloat16), "feat", axis=1, tiled=True)
    pre_coarse = jnp.dot(coarse_in, coarse_weight, preferred_element_type=jnp.float32)
    coarse_out = jax.nn.silu(pre_coarse).astype(jnp.bfloat16)
    level_two = (
        level_one
        + jnp.dot(coarse_match.astype(jnp.bfloat16), coarse_out, preferred_element_type=jnp.float32)
    ).astype(jnp.bfloat16)
    reply_rows = jnp.dot(node_match, level_two, preferred_element_type=jnp.float32).astype(
        jnp.bfloat16
    )
    returned = route_block(reply_rows, mesh_count, tile_count, "reply")
    merged = (
        hidden.astype(jnp.float32)
        + jnp.einsum("sr,sh->rh", dispatch, returned, preferred_element_type=jnp.float32)
    ).astype(jnp.bfloat16)
    pred_part = jnp.dot(merged, decode_weight, preferred_element_type=jnp.float32)
    prediction = lax.psum(pred_part, "feat")
    decode_grad = jnp.dot(merged.astype(jnp.float32).T, cotangent, precision=highest)
    grad_merged = jnp.dot(cotangent, decode_weight.astype(jnp.float32).T, precision=highest)
    grad_out = jnp.dot(
        dispatch, grad_merged.astype(jnp.bfloat16), preferred_element_type=jnp.float32
    ).astype(jnp.bfloat16)
    grad_in = route_block(grad_out, mesh_count, tile_count, "gradient")
    grad_two = jnp.einsum("sn,sh->nh", node_match, grad_in, preferred_element_type=jnp.float32)
    coarse_grad_part = jnp.dot(coarse_match.T, grad_two, precision=highest)
    grad_coarse_out = lax.psum(coarse_grad_part, ("mesh", "tile"))
    grad_pre_coarse = grad_coarse_out * silu_grad(pre_coarse)
    coarse_grad = jnp.dot(coarse_in.astype(jnp.float32).T, grad_pre_coarse, precision=highest)
    grad_coarse_full = jnp.dot(
        grad_pre_coarse, coarse_weight.astype(jnp.float32).T, precision=highest
    )
    grad_coarse_in = lax.psum_scatter(grad_coarse_full, "feat", scatter_dimension=1, tiled=True)
    grad_one = grad_two + jnp.dot(coarse_match, grad_coarse_in, precision=highest)
    grad_pre_mesh = grad_one * silu_grad(pre_mesh)
    process_grad = jnp.dot(agg_full.astype(jnp.float32).T, grad_pre_mesh, precision=highest)
    grad_pre_full = lax.all_gather(grad_pre_mesh, "feat", axis=1, tiled=True)
    weight_full = lax.all_gather(process_weight, "feat", axis=1, tiled=True)
    own_rows = lax.dynamic_slice_in_dim(
        weight_full, lax.axis_index("feat") * feat_width, feat_width, 0
    )
    grad_agg = jnp.dot(grad_pre_full, own_rows.astype(jnp.float32).T, precision=highest).astype(
        jnp.bfloat16
    )
    padded_grad = padded(
        grad_agg.reshape(patch_rows, patch_cols, feat_width), (("mesh", 0), ("tile", 1)), 2
    )
    spread = jnp.zeros((patch_rows, patch_cols, feat_width), jnp.float32)
    for code_index in range(25):
        step_x = code_index // 5 - 2
        step_y = code_index % 5 - 2
        weight_there = padded_counts[
            2 - step_x : 2 - step_x + patch_rows,
            2 - step_y : 2 - step_y + patch_cols,
            code_index : code_index + 1,
        ].astype(jnp.float32)
        spread = spread + weight_there * padded_grad[
            2 - step_x : 2 - step_x + patch_rows, 2 - step_y : 2 - step_y + patch_cols
        ].astype(jnp.float32)
    grad_zero = (grad_one + spread.reshape(nodes_local, feat_width)).astype(jnp.bfloat16)
    back_rows = jnp.dot(node_match, grad_zero, preferred_element_type=jnp.float32).astype(
        jnp.bfloat16
    )
    grad_back = route_block(back_rows, mesh_count, tile_count, "return")
    grad_hidden = grad_merged + jnp.einsum(
        "sr,sh->rh", dispatch, grad_back, preferred_element_type=jnp.float32
    )
    grad_pre_encode = grad_hidden * silu_grad(pre_encode)
    encode_grad = jnp.dot(fields.astype(jnp.float32).T, grad_pre_encode, precision=highest)
    encode_grad, process_grad, decode_grad = lax.psum(
        (encode_grad, process_grad, decode_grad), ("mesh", "tile")
    )
    return (prediction, encode_grad, process_grad, coarse_grad, decode_grad)


MESH = pl.DeviceIdType.MESH
ROW_DIMS = (((0,), (0,)), ((), ()))
COL_DIMS = (((1,), (1,)), ((), ()))
EXTRA = 16


def gather_kernel(
    mesh_count, tile_count,
    packed, enc, proc, coarse, dec,
    gath, enc_o, proc_o, coarse_o, dec_o,
    send_sem, recv_sem, pass_send, pass_recv, weight_send, weight_recv, own_sem,
):
    groups = mesh_count * tile_count
    me = lax.axis_index("mesh") * tile_count + lax.axis_index("tile")
    feat = lax.axis_index("feat")
    sibling = {"feat": 1 - feat}

    def place(group):
        return {"mesh": group // tile_count, "tile": group % tile_count}

    barrier = pltpu.get_barrier_semaphore()
    pl.semaphore_signal(barrier, inc=1, device_id=sibling, device_id_type=MESH)
    for d in range(1, groups):
        pl.semaphore_signal(
            barrier, inc=1, device_id=place((me + d) % groups), device_id_type=MESH
        )
    pl.semaphore_wait(barrier, groups)
    sends = []
    for d in range(1, groups):
        copy = pltpu.make_async_remote_copy(
            src_ref=packed.at[feat], dst_ref=gath.at[me, feat],
            send_sem=send_sem.at[d], recv_sem=recv_sem.at[d],
            device_id=place((me + d) % groups), device_id_type=MESH,
        )
        copy.start()
        sends.append(copy)
    own = pltpu.make_async_copy(packed, gath.at[me], own_sem)
    own.start()
    pairs = ((enc, enc_o), (dec, dec_o), (proc, proc_o), (coarse, coarse_o))
    weights = []
    for i, (src, dst) in enumerate(pairs):
        copy = pltpu.make_async_remote_copy(
            src_ref=src, dst_ref=dst,
            send_sem=weight_send.at[i], recv_sem=weight_recv.at[i],
            device_id=sibling, device_id_type=MESH,
        )
        copy.start()
        weights.append(copy)
    passes = []
    for d in range(1, groups):
        sends[d - 1].wait_recv()
        came = (me - d + groups) % groups
        copy = pltpu.make_async_remote_copy(
            src_ref=gath.at[came, feat], dst_ref=gath.at[came, feat],
            send_sem=pass_send.at[d], recv_sem=pass_recv.at[d],
            device_id=sibling, device_id_type=MESH,
        )
        copy.start()
        passes.append(copy)
    own.wait()
    for copy in sends:
        copy.wait_send()
    for copy in weights + passes:
        copy.wait()


def step_kernel(
    groups, tile_count, nodes, coarse_count,
    gath, enc_n, proc_n, coarse_n, dec_n, enc_o, proc_o, coarse_o, dec_o,
    prediction, encode_grad, process_grad, coarse_grad, decode_grad,
    enc, proc, coarse, dec, pre_s, hid_s, one_s, two_s, gpm_s, gpc_s,
):
    f32, b16 = jnp.float32, jnp.bfloat16
    me = lax.axis_index("mesh") * tile_count + lax.axis_index("tile")
    feat = lax.axis_index("feat")
    half = enc_n.shape[1]
    mine = pl.ds(pl.multiple_of(feat * half, half), half)
    other = pl.ds(pl.multiple_of((1 - feat) * half, half), half)
    for full, near, far in ((enc, enc_n, enc_o), (proc, proc_n, proc_o), (coarse, coarse_n, coarse_o)):
        full[:, mine] = near[...]
        full[:, other] = far[...]
    dec[mine, :] = dec_n[...]
    dec[other, :] = dec_o[...]

    c_in = enc_n.shape[0]
    part_rows = gath.shape[2] - EXTRA
    row_count = 2 * part_rows

    def dot(a, b):
        return jnp.dot(a, b, preferred_element_type=f32)

    def row_dot(a, b):
        return lax.dot_general(a, b, ROW_DIMS, preferred_element_type=f32)

    def col_dot(a, b):
        return lax.dot_general(a, b, COL_DIMS, preferred_element_type=f32)

    def onehot(ids, count):
        numbers = lax.broadcasted_iota(jnp.int32, (count, ids.shape[1]), 0)
        return jnp.where(numbers == ids, 1.0, 0.0)

    def targets(group):
        return gath[group, 0, part_rows:, :][:1, :row_count].astype(f32).astype(jnp.int32)

    pieces = [gath[g, h, :part_rows, :] for g in range(groups) for h in range(2)]
    cells = jnp.concatenate([p[:, :c_in] for p in pieces], axis=0)
    cot = jnp.concatenate([p[:, c_in:] for p in pieces], axis=0)
    attach = jnp.concatenate(
        [onehot(targets(g), nodes).astype(b16) for g in range(groups)], axis=1
    )
    extra = gath[0, 1, part_rows:, :].astype(f32)
    for g in range(1, groups):
        extra = extra + gath[g, 1, part_rows:, :].astype(f32)
    ids = extra[:, :nodes].astype(jnp.int32)
    edges = onehot(ids[0:1], nodes)
    for k in range(1, 8):
        edges = edges + onehot(ids[k : k + 1], nodes)
    edges = edges.astype(b16)
    to_coarse = onehot(ids[8:9], coarse_count).astype(b16)

    pre = dot(cells, enc[...])
    pre_s[...] = pre
    hidden = (pre * jax.nn.sigmoid(pre)).astype(b16)
    hid_s[...] = hidden
    node_in = dot(attach, hidden).astype(b16)
    node_cot = dot(attach, cot).astype(b16)
    agg = row_dot(edges, node_in).astype(b16)
    pre_mesh = dot(agg, proc[...])
    sig_mesh = jax.nn.sigmoid(pre_mesh)
    level_one = node_in.astype(f32) + pre_mesh * sig_mesh
    upper = level_one.astype(b16)
    lower = (level_one - upper.astype(f32)).astype(b16)
    coarse_in = (dot(to_coarse, upper) + dot(to_coarse, lower)).astype(b16)
    pre_coarse = dot(coarse_in, coarse[...])
    sig_coarse = jax.nn.sigmoid(pre_coarse)
    coarse_out = (pre_coarse * sig_coarse).astype(b16)
    level_two = (level_one + row_dot(to_coarse, coarse_out)).astype(b16)
    two_s[...] = level_two

    own_cells = jnp.concatenate([gath[me, h, :part_rows, :c_in] for h in range(2)], axis=0)
    own_attach = onehot(targets(me), nodes).astype(b16)
    own_pre = dot(own_cells, enc[...])
    own_hidden = (own_pre * jax.nn.sigmoid(own_pre)).astype(b16)
    merged = (own_hidden.astype(f32) + row_dot(own_attach, level_two)).astype(b16)
    prediction[...] = dot(merged, dec[...])
    decode_grad[...] = row_dot(hid_s[:, mine], cot) + row_dot(two_s[:, mine], node_cot)

    grad_two = col_dot(node_cot, dec[...])
    coarse_cot = dot(to_coarse, node_cot).astype(b16)
    grad_coarse_out = col_dot(coarse_cot, dec[...])
    grad_pre_coarse = grad_coarse_out * (
        sig_coarse * (1.0 + pre_coarse * (1.0 - sig_coarse))
    )
    gpc = grad_pre_coarse.astype(b16)
    gpc_s[...] = gpc
    coarse_grad[...] = row_dot(coarse_in, gpc_s[:, mine])
    grad_coarse_in = col_dot(gpc, coarse[...]).astype(b16)
    grad_one = grad_two + row_dot(to_coarse, grad_coarse_in)
    one_s[...] = grad_one
    gpm = (grad_one * (sig_mesh * (1.0 + pre_mesh * (1.0 - sig_mesh)))).astype(b16)
    gpm_s[...] = gpm
    process_grad[...] = row_dot(agg, gpm_s[:, mine])
    grad_agg = col_dot(gpm, proc[mine, :]).astype(b16)
    grad_zero = (one_s[:, mine] + dot(edges, grad_agg)).astype(b16)
    grad_hidden = col_dot(cot, dec[mine, :]) + row_dot(attach, grad_zero)
    pre_own = pre_s[:, mine]
    sig_own = jax.nn.sigmoid(pre_own)
    grad_pre = (grad_hidden * (sig_own * (1.0 + pre_own * (1.0 - sig_own)))).astype(b16)
    encode_grad[...] = row_dot(cells, grad_pre)


def replicated_body(
    fields, owner_group, owner_node, stencil_codes, coarse_ids,
    encode_weight, process_weight, coarse_weight, decode_weight, cotangent,
):
    f32, b16 = jnp.float32, jnp.bfloat16
    mesh_count, tile_count = lax.axis_size("mesh"), lax.axis_size("tile")
    groups = mesh_count * tile_count
    nodes_local = MA * MB
    nodes = nodes_local * groups
    m, t = lax.axis_index("mesh"), lax.axis_index("tile")
    me = m * tile_count + t
    row_count, c_in = fields.shape
    c_out = cotangent.shape[1]
    width = c_in + c_out
    half = encode_weight.shape[1]
    full = process_weight.shape[0]

    target = owner_group[:, 0] * nodes_local + owner_node
    local = jnp.arange(nodes_local, dtype=jnp.int32)[None, :]
    codes = stencil_codes.T
    row = (m * MA + local // MB + codes // 5 - 2) % (mesh_count * MA)
    col = (t * MB + local % MB + codes % 5 - 2) % (tile_count * MB)
    near = (row // MA * tile_count + col // MB) * nodes_local + row % MA * MB + col % MB
    ids = jnp.concatenate(
        [near, coarse_ids[None, :], jnp.zeros((EXTRA - 9, nodes_local), jnp.int32)], axis=0
    )
    lanes = jnp.arange(width, dtype=jnp.int32)[None, :] // nodes_local
    spread = jnp.where(lanes == me, jnp.tile(ids, (1, width // nodes_local)), 0).astype(b16)
    named = jnp.pad(target[None, :], ((0, EXTRA - 1), (0, width - row_count))).astype(b16)
    both = jnp.concatenate([fields, cotangent.astype(b16)], axis=1)
    part_rows = row_count // 2
    packed = jnp.stack(
        [
            jnp.concatenate([both[:part_rows], named], axis=0),
            jnp.concatenate([both[part_rows:], spread], axis=0),
        ]
    )
    any_spec = pl.BlockSpec(memory_space=pl.ANY)
    vmem = pl.BlockSpec(memory_space=pltpu.VMEM)
    like = lambda a: jax.ShapeDtypeStruct(a.shape, a.dtype)
    own = (encode_weight, process_weight, coarse_weight, decode_weight)
    gath, *others = pl.pallas_call(
        functools.partial(gather_kernel, mesh_count, tile_count),
        out_shape=[jax.ShapeDtypeStruct((groups,) + packed.shape, b16)] + [like(w) for w in own],
        in_specs=[vmem] + [any_spec] * 4,
        out_specs=[any_spec] * 5,
        scratch_shapes=[pltpu.SemaphoreType.DMA((groups,))] * 4
        + [pltpu.SemaphoreType.DMA((4,))] * 2
        + [pltpu.SemaphoreType.DMA],
        compiler_params=pltpu.CompilerParams(collective_id=0, has_side_effects=True),
        name="gather",
    )(packed, *own)
    coarse_count = CPD * groups
    total_rows = row_count * groups
    shape = lambda *dims: jax.ShapeDtypeStruct(dims, f32)
    return tuple(
        pl.pallas_call(
            functools.partial(step_kernel, groups, tile_count, nodes, coarse_count),
            out_shape=[
                shape(row_count, c_out), shape(c_in, half), shape(full, half),
                shape(full, half), shape(half, c_out),
            ],
            in_specs=[vmem] * 9,
            out_specs=[vmem] * 5,
            scratch_shapes=[
                pltpu.VMEM((c_in, full), b16),
                pltpu.VMEM((full, full), b16),
                pltpu.VMEM((full, full), b16),
                pltpu.VMEM((full, c_out), b16),
                pltpu.VMEM((total_rows, full), f32),
                pltpu.VMEM((total_rows, full), b16),
                pltpu.VMEM((nodes, full), f32),
                pltpu.VMEM((nodes, full), b16),
                pltpu.VMEM((nodes, full), b16),
                pltpu.VMEM((coarse_count, full), b16),
            ],
            name="step",
        )(gath, *own, *others)
    )


def solution(mesh):
    placed = (
        P(("parts", "mesh", "tile"), None),
        P(("mesh", "tile"), None),
        P(("mesh", "tile")),
        P(("mesh", "tile"), None),
        P(("mesh", "tile")),
        P(None, "feat"),
        P(None, "feat"),
        P(None, "feat"),
        P("feat", None),
        P(("parts", "mesh", "tile"), None),
    )
    groups = mesh.shape["mesh"] * mesh.shape["tile"]
    fits = MA * MB * groups <= 256
    return jax.shard_map(
        replicated_body if fits else body,
        mesh=mesh,
        in_specs=placed,
        out_specs=(
            P(("parts", "mesh", "tile"), None),
            P("parts", "feat"),
            P("parts", "feat"),
            P("parts", "feat"),
            P(("parts", "feat"), None),
        ),
        check_vma=False,
    )
```

```python
import functools

import jax
import jax.numpy as jnp
from jax import lax
from jax.experimental import pallas as pl
from jax.experimental.pallas import tpu as pltpu
from jax.sharding import PartitionSpec as P

MA = 4
MB = 8
CPD = 2


def padded(array, sides, width):
    for axis, dim in sides:
        peers, length = (lax.axis_size(axis), array.shape[dim])
        up = [(i, (i + 1) % peers) for i in range(peers)]
        down = [(j, i) for i, j in up]
        last = lax.slice_in_dim(array, length - width, length, axis=dim)
        initial = lax.slice_in_dim(array, 0, width, axis=dim)
        before = lax.ppermute(last, axis, up)
        after = lax.ppermute(initial, axis, down)
        array = jnp.concatenate([before, array, after], axis=dim)
    return array


def silu_grad(pre):
    sig = jax.nn.sigmoid(pre)
    return sig * (1.0 + pre * (1.0 - sig))


def send_rows(outgoing, slot_node):
    feat_width = outgoing.shape[-1]
    got, got_node = (
        lax.all_to_all(outgoing, ("mesh", "tile"), split_axis=0, concat_axis=0, tiled=True),
        lax.all_to_all(slot_node, ("mesh", "tile"), split_axis=0, concat_axis=0, tiled=True),
    )
    return (got.reshape(-1, feat_width), got_node.reshape(-1))


def route_block(block, mesh_count, tile_count, purpose):
    feat_width = block.shape[-1]
    slot_count = block.shape[0] // (mesh_count * tile_count)
    flat_shape = (mesh_count * tile_count, slot_count, feat_width)
    if purpose == "reply":
        moved = lax.all_to_all(
            block.reshape(flat_shape), ("mesh", "tile"), split_axis=0, concat_axis=0, tiled=True
        )
    elif purpose == "gradient":
        moved = lax.all_to_all(
            block.reshape(flat_shape), ("mesh", "tile"), split_axis=0, concat_axis=0, tiled=True
        )
    else:
        moved = lax.all_to_all(
            block.reshape(flat_shape), ("mesh", "tile"), split_axis=0, concat_axis=0, tiled=True
        )
    return moved.reshape(-1, feat_width)


def body(
    fields,
    owner_group,
    owner_node,
    stencil_codes,
    coarse_ids,
    encode_weight,
    process_weight,
    coarse_weight,
    decode_weight,
    cotangent,
):
    highest = lax.Precision.HIGHEST
    row_count = fields.shape[0]
    mesh_count = lax.axis_size("mesh")
    tile_count = lax.axis_size("tile")
    groups = mesh_count * tile_count
    slot_count = 2 * row_count // groups
    feat_width = encode_weight.shape[1]
    patch_rows = MA
    patch_cols = MB
    nodes_local = patch_rows * patch_cols
    coarse_count = CPD * groups
    target = owner_group[:, 0]
    group_onehot = (target[:, None] == jnp.arange(groups, dtype=jnp.int32)[None, :]).astype(
        jnp.int32
    )
    earlier = jnp.cumsum(group_onehot, axis=0) - group_onehot
    position = target * slot_count + jnp.sum(earlier * group_onehot, axis=1)
    matches = jnp.arange(groups * slot_count, dtype=jnp.int32)[:, None] == position[None, :]
    dispatch = matches.astype(jnp.bfloat16)
    slot_node = (jnp.max(jnp.where(matches, owner_node[None, :] + 1, 0), axis=1) - 1).reshape(
        groups, slot_count
    )
    pre_encode = jnp.dot(fields, encode_weight, preferred_element_type=jnp.float32)
    hidden = jax.nn.silu(pre_encode).astype(jnp.bfloat16)
    outgoing = jnp.dot(dispatch, hidden, preferred_element_type=jnp.float32).astype(jnp.bfloat16)
    incoming, incoming_node = send_rows(outgoing.reshape(groups, slot_count, feat_width), slot_node)
    node_match = (
        incoming_node[:, None] == jnp.arange(nodes_local, dtype=jnp.int32)[None, :]
    ).astype(jnp.bfloat16)
    node_in = jnp.einsum(
        "sn,sh->nh", node_match, incoming, preferred_element_type=jnp.float32
    ).astype(jnp.bfloat16)
    counts = jnp.sum(
        (stencil_codes[:, :, None] == jnp.arange(25, dtype=jnp.int32)[None, None, :]).astype(
            jnp.float32
        ),
        axis=1,
    )
    counts = counts.astype(jnp.bfloat16).reshape(patch_rows, patch_cols, 25)
    padded_nodes, padded_counts = (
        padded(node_in.reshape(patch_rows, patch_cols, feat_width), (("mesh", 0), ("tile", 1)), 2),
        padded(counts, (("mesh", 0), ("tile", 1)), 2),
    )
    gathered = jnp.zeros((patch_rows, patch_cols, feat_width), jnp.float32)
    for code_index in range(25):
        step_x = code_index // 5 - 2
        step_y = code_index % 5 - 2
        weight_here = padded_counts[
            2 : 2 + patch_rows, 2 : 2 + patch_cols, code_index : code_index + 1
        ].astype(jnp.float32)
        gathered = gathered + weight_here * padded_nodes[
            2 + step_x : 2 + step_x + patch_rows, 2 + step_y : 2 + step_y + patch_cols
        ].astype(jnp.float32)
    agg = gathered.reshape(nodes_local, feat_width).astype(jnp.bfloat16)
    agg_full = lax.all_gather(agg, "feat", axis=1, tiled=True)
    pre_mesh = jnp.dot(agg_full, process_weight, preferred_element_type=jnp.float32)
    level_one = node_in.astype(jnp.float32) + jax.nn.silu(pre_mesh)
    coarse_match = (
        coarse_ids[:, None] == jnp.arange(coarse_count, dtype=jnp.int32)[None, :]
    ).astype(jnp.float32)
    coarse_part = jnp.dot(coarse_match.T, level_one, precision=highest)
    coarse_total = lax.psum(coarse_part, ("mesh", "tile"))
    coarse_in = lax.all_gather(coarse_total.astype(jnp.bfloat16), "feat", axis=1, tiled=True)
    pre_coarse = jnp.dot(coarse_in, coarse_weight, preferred_element_type=jnp.float32)
    coarse_out = jax.nn.silu(pre_coarse).astype(jnp.bfloat16)
    level_two = (
        level_one
        + jnp.dot(coarse_match.astype(jnp.bfloat16), coarse_out, preferred_element_type=jnp.float32)
    ).astype(jnp.bfloat16)
    reply_rows = jnp.dot(node_match, level_two, preferred_element_type=jnp.float32).astype(
        jnp.bfloat16
    )
    returned = route_block(reply_rows, mesh_count, tile_count, "reply")
    merged = (
        hidden.astype(jnp.float32)
        + jnp.einsum("sr,sh->rh", dispatch, returned, preferred_element_type=jnp.float32)
    ).astype(jnp.bfloat16)
    pred_part = jnp.dot(merged, decode_weight, preferred_element_type=jnp.float32)
    prediction = lax.psum(pred_part, "feat")
    decode_grad = jnp.dot(merged.astype(jnp.float32).T, cotangent, precision=highest)
    grad_merged = jnp.dot(cotangent, decode_weight.astype(jnp.float32).T, precision=highest)
    grad_out = jnp.dot(
        dispatch, grad_merged.astype(jnp.bfloat16), preferred_element_type=jnp.float32
    ).astype(jnp.bfloat16)
    grad_in = route_block(grad_out, mesh_count, tile_count, "gradient")
    grad_two = jnp.einsum("sn,sh->nh", node_match, grad_in, preferred_element_type=jnp.float32)
    coarse_grad_part = jnp.dot(coarse_match.T, grad_two, precision=highest)
    grad_coarse_out = lax.psum(coarse_grad_part, ("mesh", "tile"))
    grad_pre_coarse = grad_coarse_out * silu_grad(pre_coarse)
    coarse_grad = jnp.dot(coarse_in.astype(jnp.float32).T, grad_pre_coarse, precision=highest)
    grad_coarse_full = jnp.dot(
        grad_pre_coarse, coarse_weight.astype(jnp.float32).T, precision=highest
    )
    grad_coarse_in = lax.psum_scatter(grad_coarse_full, "feat", scatter_dimension=1, tiled=True)
    grad_one = grad_two + jnp.dot(coarse_match, grad_coarse_in, precision=highest)
    grad_pre_mesh = grad_one * silu_grad(pre_mesh)
    process_grad = jnp.dot(agg_full.astype(jnp.float32).T, grad_pre_mesh, precision=highest)
    grad_pre_full = lax.all_gather(grad_pre_mesh, "feat", axis=1, tiled=True)
    weight_full = lax.all_gather(process_weight, "feat", axis=1, tiled=True)
    own_rows = lax.dynamic_slice_in_dim(
        weight_full, lax.axis_index("feat") * feat_width, feat_width, 0
    )
    grad_agg = jnp.dot(grad_pre_full, own_rows.astype(jnp.float32).T, precision=highest).astype(
        jnp.bfloat16
    )
    padded_grad = padded(
        grad_agg.reshape(patch_rows, patch_cols, feat_width), (("mesh", 0), ("tile", 1)), 2
    )
    spread = jnp.zeros((patch_rows, patch_cols, feat_width), jnp.float32)
    for code_index in range(25):
        step_x = code_index // 5 - 2
        step_y = code_index % 5 - 2
        weight_there = padded_counts[
            2 - step_x : 2 - step_x + patch_rows,
            2 - step_y : 2 - step_y + patch_cols,
            code_index : code_index + 1,
        ].astype(jnp.float32)
        spread = spread + weight_there * padded_grad[
            2 - step_x : 2 - step_x + patch_rows, 2 - step_y : 2 - step_y + patch_cols
        ].astype(jnp.float32)
    grad_zero = (grad_one + spread.reshape(nodes_local, feat_width)).astype(jnp.bfloat16)
    back_rows = jnp.dot(node_match, grad_zero, preferred_element_type=jnp.float32).astype(
        jnp.bfloat16
    )
    grad_back = route_block(back_rows, mesh_count, tile_count, "return")
    grad_hidden = grad_merged + jnp.einsum(
        "sr,sh->rh", dispatch, grad_back, preferred_element_type=jnp.float32
    )
    grad_pre_encode = grad_hidden * silu_grad(pre_encode)
    encode_grad = jnp.dot(fields.astype(jnp.float32).T, grad_pre_encode, precision=highest)
    encode_grad, process_grad, decode_grad = lax.psum(
        (encode_grad, process_grad, decode_grad), ("mesh", "tile")
    )
    return (prediction, encode_grad, process_grad, coarse_grad, decode_grad)


MESH = pl.DeviceIdType.MESH
ROW_DIMS = (((0,), (0,)), ((), ()))
COL_DIMS = (((1,), (1,)), ((), ()))
EXTRA = 8


def quotient(values, divisor):
    return jnp.floor((values.astype(jnp.float32) + 0.5) * (1.0 / divisor)).astype(jnp.int32)


def onehot(ids, count):
    numbers = lax.broadcasted_iota(jnp.int32, (count, ids.shape[1]), 0)
    return jnp.where(numbers == ids, 1.0, 0.0)


def dot(a, b):
    return jnp.dot(a, b, preferred_element_type=jnp.float32)


def row_dot(a, b):
    return lax.dot_general(a, b, ROW_DIMS, preferred_element_type=jnp.float32)


def col_dot(a, b):
    return lax.dot_general(a, b, COL_DIMS, preferred_element_type=jnp.float32)


def step_kernel(
    mesh_count, tile_count,
    fields, owner_group, owner_node, codes, coarse_ids, cotangent,
    enc_n, proc_n, coarse_n, dec_n,
    prediction, encode_grad, process_grad, coarse_grad, decode_grad,
    gath, enc, proc, coarse, dec, cells, cot, attach, pre_s, hid_s, base_s, one_s, two_s, gpm_s, gpc_s,
    send_sem, recv_sem, pass_send, pass_recv, weight_send, weight_recv, local_sem,
):
    f32, b16 = jnp.float32, jnp.bfloat16
    groups = mesh_count * tile_count
    m, t, feat = lax.axis_index("mesh"), lax.axis_index("tile"), lax.axis_index("feat")
    me = m * tile_count + t
    sibling = {"feat": 1 - feat}
    nodes_local = MA * MB
    nodes = nodes_local * groups
    coarse_count = CPD * groups
    row_count, c_in = fields.shape
    width = c_in + cotangent.shape[1]
    part_rows = row_count // 2
    half = enc_n.shape[1]
    mine = pl.ds(pl.multiple_of(feat * half, half), half)

    def place(group):
        return {"mesh": group // tile_count, "tile": group % tile_count}

    barrier = pltpu.get_barrier_semaphore()
    pl.semaphore_signal(barrier, inc=1, device_id=sibling, device_id_type=MESH)
    for d in range(1, groups):
        pl.semaphore_signal(
            barrier, inc=1, device_id=place((me + d) % groups), device_id_type=MESH
        )

    pairs = (
        (enc_n, enc.at[:, mine]), (dec_n, dec.at[mine, :]),
        (proc_n, proc.at[:, mine]), (coarse_n, coarse.at[:, mine]),
    )
    locals_ = []
    for i, (src, dst) in enumerate(pairs):
        copy = pltpu.make_async_copy(src, dst, local_sem.at[i])
        copy.start()
        locals_.append(copy)

    both = jnp.concatenate([fields[...], cotangent[...].astype(b16)], axis=1)
    gath[me, 0, :part_rows, :] = both[:part_rows]
    gath[me, 1, :part_rows, :] = both[part_rows:]
    code = codes[...]
    code_row = sum(jnp.where(code >= 5 * i, 1, 0) for i in range(1, 5))
    local = lax.broadcasted_iota(jnp.int32, (1, nodes_local), 1)
    local_row = quotient(local, MB)
    row = m * MA + local_row + code_row - 2
    col = t * MB + (local - local_row * MB) + (code - 5 * code_row) - 2
    rows_all, cols_all = mesh_count * MA, tile_count * MB
    for _ in range(2):
        row = jnp.where(row < 0, row + rows_all, jnp.where(row >= rows_all, row - rows_all, row))
        col = jnp.where(col < 0, col + cols_all, jnp.where(col >= cols_all, col - cols_all, col))
    row_group, col_group = quotient(row, MA), quotient(col, MB)
    near = (
        (row_group * tile_count + col_group) * nodes_local
        + (row - row_group * MA) * MB + col - col_group * MB
    )
    spot = jnp.where(
        lax.broadcasted_iota(jnp.int32, (nodes_local, width), 1)
        == lax.broadcasted_iota(jnp.int32, (nodes_local, width), 0) + nodes_local * me,
        1.0, 0.0,
    ).astype(b16)
    order = lax.broadcasted_iota(jnp.int32, (EXTRA, nodes_local), 0)
    owned = jnp.where(order == 1, coarse_ids[...], 0).astype(f32).astype(b16)
    owned = dot(owned, spot)
    target = (owner_group[...] * nodes_local + owner_node[...]).astype(f32)
    order = lax.broadcasted_iota(jnp.int32, (EXTRA, row_count), 0)
    named = jnp.where(order == 0, target, owned[:, :row_count])
    gath[me, 0, part_rows:, :] = jnp.concatenate([named, owned[:, row_count:]], axis=1).astype(b16)
    gath[me, 1, part_rows:, :] = dot(near.astype(f32).astype(b16), spot).astype(b16)

    pl.semaphore_wait(barrier, groups)
    sends = []
    for d in range(1, groups):
        copy = pltpu.make_async_remote_copy(
            src_ref=gath.at[me, feat], dst_ref=gath.at[me, feat],
            send_sem=send_sem.at[d], recv_sem=recv_sem.at[d],
            device_id=place((me + d) % groups), device_id_type=MESH,
        )
        copy.start()
        sends.append(copy)
    weights = []
    for i, (src, dst) in enumerate(pairs):
        copy = pltpu.make_async_remote_copy(
            src_ref=src, dst_ref=dst,
            send_sem=weight_send.at[i], recv_sem=weight_recv.at[i],
            device_id=sibling, device_id_type=MESH,
        )
        copy.start()
        weights.append(copy)

    def take(g):
        rows = pl.ds(pl.multiple_of(g * row_count, row_count), row_count)
        block = jnp.concatenate([gath[g, h, :part_rows, :] for h in range(2)], axis=0)
        x, c = block[:, :c_in], block[:, c_in:]
        cells[rows, :] = x
        cot[rows, :] = c
        ids = gath[g, 0, part_rows:, :][:1, :row_count].astype(f32).astype(jnp.int32)
        attach[:, rows] = onehot(ids, nodes).astype(b16)
        pre = dot(x, enc[...])
        pre_s[rows, :] = pre
        hid_s[rows, :] = (pre * jax.nn.sigmoid(pre)).astype(b16)
        base_s[rows, :] = col_dot(c, dec[mine, :])

    for i in range(2):
        locals_[i].wait()
        weights[i].wait_recv()
    passes = []
    take(me)
    for d in range(1, groups):
        sends[d - 1].wait_recv()
        came = (me - d + groups) % groups
        copy = pltpu.make_async_remote_copy(
            src_ref=gath.at[came, feat], dst_ref=gath.at[came, feat],
            send_sem=pass_send.at[d], recv_sem=pass_recv.at[d],
            device_id=sibling, device_id_type=MESH,
        )
        copy.start()
        passes.append(copy)
        if d > 1:
            passes[d - 2].wait_recv()
            take((me - d + 1 + groups) % groups)
    passes[groups - 2].wait_recv()
    take((me + 1) % groups)

    node_in = dot(attach[...], hid_s[...]).astype(b16)
    node_cot = dot(attach[...], cot[...]).astype(b16)
    owned = gath[0, 0, part_rows:, :].astype(f32)
    linked = gath[0, 1, part_rows:, :].astype(f32)
    for g in range(1, groups):
        owned = owned + gath[g, 0, part_rows:, :].astype(f32)
        linked = linked + gath[g, 1, part_rows:, :].astype(f32)
    linked = linked[:, :nodes].astype(jnp.int32)
    edges = onehot(linked[0:1], nodes)
    for k in range(1, linked.shape[0]):
        edges = edges + onehot(linked[k : k + 1], nodes)
    edges = edges.astype(b16)
    to_coarse = onehot(owned[1:2, :nodes].astype(jnp.int32), coarse_count).astype(b16)

    agg = row_dot(edges, node_in).astype(b16)
    locals_[2].wait()
    weights[2].wait_recv()
    pre_mesh = dot(agg, proc[...])
    sig_mesh = jax.nn.sigmoid(pre_mesh)
    level_one = node_in.astype(f32) + pre_mesh * sig_mesh
    upper = level_one.astype(b16)
    lower = (level_one - upper.astype(f32)).astype(b16)
    coarse_in = (dot(to_coarse, upper) + dot(to_coarse, lower)).astype(b16)
    locals_[3].wait()
    weights[3].wait_recv()
    pre_coarse = dot(coarse_in, coarse[...])
    sig_coarse = jax.nn.sigmoid(pre_coarse)
    coarse_out = (pre_coarse * sig_coarse).astype(b16)
    level_two = (level_one + row_dot(to_coarse, coarse_out)).astype(b16)
    two_s[...] = level_two

    own_rows = pl.ds(pl.multiple_of(me * row_count, row_count), row_count)
    merged = (
        hid_s[own_rows, :].astype(f32) + row_dot(attach[:, own_rows], level_two)
    ).astype(b16)
    prediction[...] = dot(merged, dec[...])
    decode_grad[...] = row_dot(hid_s[:, mine], cot[...]) + row_dot(two_s[:, mine], node_cot)

    grad_two = col_dot(node_cot, dec[...])
    coarse_cot = dot(to_coarse, node_cot).astype(b16)
    grad_coarse_out = col_dot(coarse_cot, dec[...])
    grad_pre_coarse = grad_coarse_out * (
        sig_coarse * (1.0 + pre_coarse * (1.0 - sig_coarse))
    )
    gpc = grad_pre_coarse.astype(b16)
    gpc_s[...] = gpc
    coarse_grad[...] = row_dot(coarse_in, gpc_s[:, mine])
    grad_coarse_in = col_dot(gpc, coarse[...]).astype(b16)
    grad_one = grad_two + row_dot(to_coarse, grad_coarse_in)
    one_s[...] = grad_one
    gpm = (grad_one * (sig_mesh * (1.0 + pre_mesh * (1.0 - sig_mesh)))).astype(b16)
    gpm_s[...] = gpm
    process_grad[...] = row_dot(agg, gpm_s[:, mine])
    grad_agg = col_dot(gpm, proc[mine, :]).astype(b16)
    grad_zero = (one_s[:, mine] + dot(edges, grad_agg)).astype(b16)
    grad_hidden = base_s[...] + row_dot(attach[...], grad_zero)
    pre_own = pre_s[:, mine]
    sig_own = jax.nn.sigmoid(pre_own)
    grad_pre = (grad_hidden * (sig_own * (1.0 + pre_own * (1.0 - sig_own)))).astype(b16)
    encode_grad[...] = row_dot(cells[...], grad_pre)

    for copy in sends + passes + weights:
        copy.wait_send()


def replicated_body(
    fields, owner_group, owner_node, stencil_codes, coarse_ids,
    encode_weight, process_weight, coarse_weight, decode_weight, cotangent,
):
    f32, b16 = jnp.float32, jnp.bfloat16
    mesh_count, tile_count = lax.axis_size("mesh"), lax.axis_size("tile")
    groups = mesh_count * tile_count
    nodes = MA * MB * groups
    row_count, c_in = fields.shape
    c_out = cotangent.shape[1]
    half = encode_weight.shape[1]
    full = process_weight.shape[0]
    coarse_count = CPD * groups
    total_rows = row_count * groups
    any_spec = pl.BlockSpec(memory_space=pl.ANY)
    vmem = pl.BlockSpec(memory_space=pltpu.VMEM)
    shape = lambda *dims: jax.ShapeDtypeStruct(dims, f32)
    return tuple(
        pl.pallas_call(
            functools.partial(step_kernel, mesh_count, tile_count),
            out_shape=[
                shape(row_count, c_out), shape(c_in, half), shape(full, half),
                shape(full, half), shape(half, c_out),
            ],
            in_specs=[vmem] * 6 + [any_spec] * 4,
            out_specs=[vmem] * 5,
            scratch_shapes=[
                pltpu.VMEM((groups, 2, row_count // 2 + EXTRA, c_in + c_out), b16),
                pltpu.VMEM((c_in, full), b16),
                pltpu.VMEM((full, full), b16),
                pltpu.VMEM((full, full), b16),
                pltpu.VMEM((full, c_out), b16),
                pltpu.VMEM((total_rows, c_in), b16),
                pltpu.VMEM((total_rows, c_out), b16),
                pltpu.VMEM((nodes, total_rows), b16),
                pltpu.VMEM((total_rows, full), f32),
                pltpu.VMEM((total_rows, full), b16),
                pltpu.VMEM((total_rows, half), f32),
                pltpu.VMEM((nodes, full), f32),
                pltpu.VMEM((nodes, full), b16),
                pltpu.VMEM((nodes, full), b16),
                pltpu.VMEM((coarse_count, full), b16),
            ]
            + [pltpu.SemaphoreType.DMA((groups,))] * 4
            + [pltpu.SemaphoreType.DMA((4,))] * 3,
            compiler_params=pltpu.CompilerParams(collective_id=0, has_side_effects=True),
            name="step",
        )(
            fields, owner_group.reshape(1, -1), owner_node.reshape(1, -1),
            stencil_codes.T, coarse_ids.reshape(1, -1), cotangent,
            encode_weight, process_weight, coarse_weight, decode_weight,
        )
    )


def any_size(*args):
    groups = lax.axis_size("mesh") * lax.axis_size("tile")
    row_count, c_in = args[0].shape
    nodes = MA * MB * groups
    aligned = row_count % 128 == 0 and args[3].shape[1] == EXTRA
    fits = nodes <= min(256, c_in + args[9].shape[1]) and aligned and lax.axis_size("feat") == 2
    return (replicated_body if fits else body)(*args)


def solution(mesh):
    placed = (
        P(("parts", "mesh", "tile"), None),
        P(("mesh", "tile"), None),
        P(("mesh", "tile")),
        P(("mesh", "tile"), None),
        P(("mesh", "tile")),
        P(None, "feat"),
        P(None, "feat"),
        P(None, "feat"),
        P("feat", None),
        P(("parts", "mesh", "tile"), None),
    )
    return jax.shard_map(
        any_size,
        mesh=mesh,
        in_specs=placed,
        out_specs=(
            P(("parts", "mesh", "tile"), None),
            P("parts", "feat"),
            P("parts", "feat"),
            P("parts", "feat"),
            P(("parts", "feat"), None),
        ),
        check_vma=False,
    )
```

```python
import functools

import jax
import jax.numpy as jnp
from jax import lax
from jax.experimental import pallas as pl
from jax.experimental.pallas import tpu as pltpu
from jax.sharding import PartitionSpec as P

MA = 4
MB = 8
CPD = 2


def padded(array, sides, width):
    for axis, dim in sides:
        peers, length = (lax.axis_size(axis), array.shape[dim])
        up = [(i, (i + 1) % peers) for i in range(peers)]
        down = [(j, i) for i, j in up]
        last = lax.slice_in_dim(array, length - width, length, axis=dim)
        initial = lax.slice_in_dim(array, 0, width, axis=dim)
        before = lax.ppermute(last, axis, up)
        after = lax.ppermute(initial, axis, down)
        array = jnp.concatenate([before, array, after], axis=dim)
    return array


def silu_grad(pre):
    sig = jax.nn.sigmoid(pre)
    return sig * (1.0 + pre * (1.0 - sig))


def send_rows(outgoing, slot_node):
    feat_width = outgoing.shape[-1]
    got, got_node = (
        lax.all_to_all(outgoing, ("mesh", "tile"), split_axis=0, concat_axis=0, tiled=True),
        lax.all_to_all(slot_node, ("mesh", "tile"), split_axis=0, concat_axis=0, tiled=True),
    )
    return (got.reshape(-1, feat_width), got_node.reshape(-1))


def route_block(block, mesh_count, tile_count, purpose):
    feat_width = block.shape[-1]
    slot_count = block.shape[0] // (mesh_count * tile_count)
    flat_shape = (mesh_count * tile_count, slot_count, feat_width)
    if purpose == "reply":
        moved = lax.all_to_all(
            block.reshape(flat_shape), ("mesh", "tile"), split_axis=0, concat_axis=0, tiled=True
        )
    elif purpose == "gradient":
        moved = lax.all_to_all(
            block.reshape(flat_shape), ("mesh", "tile"), split_axis=0, concat_axis=0, tiled=True
        )
    else:
        moved = lax.all_to_all(
            block.reshape(flat_shape), ("mesh", "tile"), split_axis=0, concat_axis=0, tiled=True
        )
    return moved.reshape(-1, feat_width)


def body(
    fields,
    owner_group,
    owner_node,
    stencil_codes,
    coarse_ids,
    encode_weight,
    process_weight,
    coarse_weight,
    decode_weight,
    cotangent,
):
    highest = lax.Precision.HIGHEST
    row_count = fields.shape[0]
    mesh_count = lax.axis_size("mesh")
    tile_count = lax.axis_size("tile")
    groups = mesh_count * tile_count
    slot_count = 2 * row_count // groups
    feat_width = encode_weight.shape[1]
    patch_rows = MA
    patch_cols = MB
    nodes_local = patch_rows * patch_cols
    coarse_count = CPD * groups
    target = owner_group[:, 0]
    group_onehot = (target[:, None] == jnp.arange(groups, dtype=jnp.int32)[None, :]).astype(
        jnp.int32
    )
    earlier = jnp.cumsum(group_onehot, axis=0) - group_onehot
    position = target * slot_count + jnp.sum(earlier * group_onehot, axis=1)
    matches = jnp.arange(groups * slot_count, dtype=jnp.int32)[:, None] == position[None, :]
    dispatch = matches.astype(jnp.bfloat16)
    slot_node = (jnp.max(jnp.where(matches, owner_node[None, :] + 1, 0), axis=1) - 1).reshape(
        groups, slot_count
    )
    pre_encode = jnp.dot(fields, encode_weight, preferred_element_type=jnp.float32)
    hidden = jax.nn.silu(pre_encode).astype(jnp.bfloat16)
    outgoing = jnp.dot(dispatch, hidden, preferred_element_type=jnp.float32).astype(jnp.bfloat16)
    incoming, incoming_node = send_rows(outgoing.reshape(groups, slot_count, feat_width), slot_node)
    node_match = (
        incoming_node[:, None] == jnp.arange(nodes_local, dtype=jnp.int32)[None, :]
    ).astype(jnp.bfloat16)
    node_in = jnp.einsum(
        "sn,sh->nh", node_match, incoming, preferred_element_type=jnp.float32
    ).astype(jnp.bfloat16)
    counts = jnp.sum(
        (stencil_codes[:, :, None] == jnp.arange(25, dtype=jnp.int32)[None, None, :]).astype(
            jnp.float32
        ),
        axis=1,
    )
    counts = counts.astype(jnp.bfloat16).reshape(patch_rows, patch_cols, 25)
    padded_nodes, padded_counts = (
        padded(node_in.reshape(patch_rows, patch_cols, feat_width), (("mesh", 0), ("tile", 1)), 2),
        padded(counts, (("mesh", 0), ("tile", 1)), 2),
    )
    gathered = jnp.zeros((patch_rows, patch_cols, feat_width), jnp.float32)
    for code_index in range(25):
        step_x = code_index // 5 - 2
        step_y = code_index % 5 - 2
        weight_here = padded_counts[
            2 : 2 + patch_rows, 2 : 2 + patch_cols, code_index : code_index + 1
        ].astype(jnp.float32)
        gathered = gathered + weight_here * padded_nodes[
            2 + step_x : 2 + step_x + patch_rows, 2 + step_y : 2 + step_y + patch_cols
        ].astype(jnp.float32)
    agg = gathered.reshape(nodes_local, feat_width).astype(jnp.bfloat16)
    agg_full = lax.all_gather(agg, "feat", axis=1, tiled=True)
    pre_mesh = jnp.dot(agg_full, process_weight, preferred_element_type=jnp.float32)
    level_one = node_in.astype(jnp.float32) + jax.nn.silu(pre_mesh)
    coarse_match = (
        coarse_ids[:, None] == jnp.arange(coarse_count, dtype=jnp.int32)[None, :]
    ).astype(jnp.float32)
    coarse_part = jnp.dot(coarse_match.T, level_one, precision=highest)
    coarse_total = lax.psum(coarse_part, ("mesh", "tile"))
    coarse_in = lax.all_gather(coarse_total.astype(jnp.bfloat16), "feat", axis=1, tiled=True)
    pre_coarse = jnp.dot(coarse_in, coarse_weight, preferred_element_type=jnp.float32)
    coarse_out = jax.nn.silu(pre_coarse).astype(jnp.bfloat16)
    level_two = (
        level_one
        + jnp.dot(coarse_match.astype(jnp.bfloat16), coarse_out, preferred_element_type=jnp.float32)
    ).astype(jnp.bfloat16)
    reply_rows = jnp.dot(node_match, level_two, preferred_element_type=jnp.float32).astype(
        jnp.bfloat16
    )
    returned = route_block(reply_rows, mesh_count, tile_count, "reply")
    merged = (
        hidden.astype(jnp.float32)
        + jnp.einsum("sr,sh->rh", dispatch, returned, preferred_element_type=jnp.float32)
    ).astype(jnp.bfloat16)
    pred_part = jnp.dot(merged, decode_weight, preferred_element_type=jnp.float32)
    prediction = lax.psum(pred_part, "feat")
    decode_grad = jnp.dot(merged.astype(jnp.float32).T, cotangent, precision=highest)
    grad_merged = jnp.dot(cotangent, decode_weight.astype(jnp.float32).T, precision=highest)
    grad_out = jnp.dot(
        dispatch, grad_merged.astype(jnp.bfloat16), preferred_element_type=jnp.float32
    ).astype(jnp.bfloat16)
    grad_in = route_block(grad_out, mesh_count, tile_count, "gradient")
    grad_two = jnp.einsum("sn,sh->nh", node_match, grad_in, preferred_element_type=jnp.float32)
    coarse_grad_part = jnp.dot(coarse_match.T, grad_two, precision=highest)
    grad_coarse_out = lax.psum(coarse_grad_part, ("mesh", "tile"))
    grad_pre_coarse = grad_coarse_out * silu_grad(pre_coarse)
    coarse_grad = jnp.dot(coarse_in.astype(jnp.float32).T, grad_pre_coarse, precision=highest)
    grad_coarse_full = jnp.dot(
        grad_pre_coarse, coarse_weight.astype(jnp.float32).T, precision=highest
    )
    grad_coarse_in = lax.psum_scatter(grad_coarse_full, "feat", scatter_dimension=1, tiled=True)
    grad_one = grad_two + jnp.dot(coarse_match, grad_coarse_in, precision=highest)
    grad_pre_mesh = grad_one * silu_grad(pre_mesh)
    process_grad = jnp.dot(agg_full.astype(jnp.float32).T, grad_pre_mesh, precision=highest)
    grad_pre_full = lax.all_gather(grad_pre_mesh, "feat", axis=1, tiled=True)
    weight_full = lax.all_gather(process_weight, "feat", axis=1, tiled=True)
    own_rows = lax.dynamic_slice_in_dim(
        weight_full, lax.axis_index("feat") * feat_width, feat_width, 0
    )
    grad_agg = jnp.dot(grad_pre_full, own_rows.astype(jnp.float32).T, precision=highest).astype(
        jnp.bfloat16
    )
    padded_grad = padded(
        grad_agg.reshape(patch_rows, patch_cols, feat_width), (("mesh", 0), ("tile", 1)), 2
    )
    spread = jnp.zeros((patch_rows, patch_cols, feat_width), jnp.float32)
    for code_index in range(25):
        step_x = code_index // 5 - 2
        step_y = code_index % 5 - 2
        weight_there = padded_counts[
            2 - step_x : 2 - step_x + patch_rows,
            2 - step_y : 2 - step_y + patch_cols,
            code_index : code_index + 1,
        ].astype(jnp.float32)
        spread = spread + weight_there * padded_grad[
            2 - step_x : 2 - step_x + patch_rows, 2 - step_y : 2 - step_y + patch_cols
        ].astype(jnp.float32)
    grad_zero = (grad_one + spread.reshape(nodes_local, feat_width)).astype(jnp.bfloat16)
    back_rows = jnp.dot(node_match, grad_zero, preferred_element_type=jnp.float32).astype(
        jnp.bfloat16
    )
    grad_back = route_block(back_rows, mesh_count, tile_count, "return")
    grad_hidden = grad_merged + jnp.einsum(
        "sr,sh->rh", dispatch, grad_back, preferred_element_type=jnp.float32
    )
    grad_pre_encode = grad_hidden * silu_grad(pre_encode)
    encode_grad = jnp.dot(fields.astype(jnp.float32).T, grad_pre_encode, precision=highest)
    encode_grad, process_grad, decode_grad = lax.psum(
        (encode_grad, process_grad, decode_grad), ("mesh", "tile")
    )
    return (prediction, encode_grad, process_grad, coarse_grad, decode_grad)


MESH = pl.DeviceIdType.MESH
ROW_DIMS = (((0,), (0,)), ((), ()))
COL_DIMS = (((1,), (1,)), ((), ()))
IDS = 8


def quotient(values, divisor):
    return jnp.floor((values.astype(jnp.float32) + 0.5) * (1.0 / divisor)).astype(jnp.int32)


def onehot(ids, count):
    numbers = lax.broadcasted_iota(jnp.int32, (count, ids.shape[1]), 0)
    return jnp.where(numbers == ids, 1.0, 0.0)


def dot(a, b):
    return jnp.dot(a, b, preferred_element_type=jnp.float32)


def row_dot(a, b):
    return lax.dot_general(a, b, ROW_DIMS, preferred_element_type=jnp.float32)


def col_dot(a, b):
    return lax.dot_general(a, b, COL_DIMS, preferred_element_type=jnp.float32)


def step_kernel(
    mesh_count, tile_count,
    fields, owner_group, owner_node, codes, coarse_ids, cotangent,
    enc_n, proc_n, coarse_n, dec_n,
    prediction, encode_grad, decode_grad, agg_out, gpm_out, coarse_in_out, gpc_out,
    gath, gath_cot, enc, proc, coarse, dec, cells, cot, attach, pre_s, hid_s, slope_s, one_s, two_s, gpm_s, gpc_s,
    send_sem, recv_sem, pass_send, pass_recv, cot_send, cot_recv, cot_pass_send, cot_pass_recv,
    weight_send, weight_recv, local_sem,
):
    f32, b16 = jnp.float32, jnp.bfloat16
    groups = mesh_count * tile_count
    m, t, feat = lax.axis_index("mesh"), lax.axis_index("tile"), lax.axis_index("feat")
    me = m * tile_count + t
    sibling = {"feat": 1 - feat}
    nodes_local = MA * MB
    nodes = nodes_local * groups
    coarse_count = CPD * groups
    row_count, c_in = fields.shape
    width = 2 * row_count
    part_rows = row_count // 2
    half = enc_n.shape[1]
    mine = pl.ds(pl.multiple_of(feat * half, half), half)

    def place(group):
        return {"mesh": group // tile_count, "tile": group % tile_count}

    barrier = pltpu.get_barrier_semaphore()
    pl.semaphore_signal(barrier, inc=1, device_id=sibling, device_id_type=MESH)
    for d in range(1, groups):
        pl.semaphore_signal(
            barrier, inc=1, device_id=place((me + d) % groups), device_id_type=MESH
        )

    pairs = (
        (enc_n, enc.at[:, mine]), (dec_n, dec.at[mine, :]),
        (proc_n, proc.at[:, mine]), (coarse_n, coarse.at[:, mine]),
    )
    locals_ = []
    for i, (src, dst) in enumerate(pairs):
        copy = pltpu.make_async_copy(src, dst, local_sem.at[i])
        copy.start()
        locals_.append(copy)

    own_cot = cotangent[...].astype(b16)
    for h in range(2):
        gath[me, h, :part_rows, :] = fields[h * part_rows : (h + 1) * part_rows, :]
        gath_cot[me, h] = own_cot[h * part_rows : (h + 1) * part_rows]
    code = codes[...]
    code_row = sum(jnp.where(code >= 5 * i, 1, 0) for i in range(1, 5))
    local = lax.broadcasted_iota(jnp.int32, (1, nodes_local), 1)
    local_row = quotient(local, MB)
    row = m * MA + local_row + code_row - 2
    col = t * MB + (local - local_row * MB) + (code - 5 * code_row) - 2
    rows_all, cols_all = mesh_count * MA, tile_count * MB
    for _ in range(2):
        row = jnp.where(row < 0, row + rows_all, jnp.where(row >= rows_all, row - rows_all, row))
        col = jnp.where(col < 0, col + cols_all, jnp.where(col >= cols_all, col - cols_all, col))
    row_group, col_group = quotient(row, MA), quotient(col, MB)
    near = (
        (row_group * tile_count + col_group) * nodes_local
        + (row - row_group * MA) * MB + col - col_group * MB
    )
    spot = jnp.where(
        lax.broadcasted_iota(jnp.int32, (nodes_local, width), 1)
        == lax.broadcasted_iota(jnp.int32, (nodes_local, width), 0) + nodes_local * me,
        1.0, 0.0,
    ).astype(b16)
    order = lax.broadcasted_iota(jnp.int32, (IDS, nodes_local), 0)
    owned = jnp.where(order == 1, coarse_ids[...], 0).astype(f32).astype(b16)
    owned = dot(owned, spot)
    target = (owner_group[...] * nodes_local + owner_node[...]).astype(f32)
    order = lax.broadcasted_iota(jnp.int32, (IDS, row_count), 0)
    named = jnp.where(order == 0, target, owned[:, :row_count])
    linked = dot(near.astype(f32).astype(b16), spot)
    gath[me, 0, part_rows:, :] = jnp.concatenate([named, owned[:, row_count:]], axis=0).astype(b16)
    gath[me, 1, part_rows:, :] = jnp.concatenate(
        [linked[:, :row_count], linked[:, row_count:]], axis=0
    ).astype(b16)

    pl.semaphore_wait(barrier, groups)

    def spread(buffer, send, recv):
        copies = []
        for d in range(1, groups):
            copy = pltpu.make_async_remote_copy(
                src_ref=buffer.at[me, feat], dst_ref=buffer.at[me, feat],
                send_sem=send.at[d], recv_sem=recv.at[d],
                device_id=place((me + d) % groups), device_id_type=MESH,
            )
            copy.start()
            copies.append(copy)
        return copies

    def hand_on(buffer, d, send, recv):
        came = (me - d + groups) % groups
        copy = pltpu.make_async_remote_copy(
            src_ref=buffer.at[came, feat], dst_ref=buffer.at[came, feat],
            send_sem=send.at[d], recv_sem=recv.at[d],
            device_id=sibling, device_id_type=MESH,
        )
        copy.start()
        return copy

    sends = spread(gath, send_sem, recv_sem)
    cot_sends = spread(gath_cot, cot_send, cot_recv)
    weights = []
    for i, (src, dst) in enumerate(pairs):
        copy = pltpu.make_async_remote_copy(
            src_ref=src, dst_ref=dst,
            send_sem=weight_send.at[i], recv_sem=weight_recv.at[i],
            device_id=sibling, device_id_type=MESH,
        )
        copy.start()
        weights.append(copy)

    def span(g):
        return pl.ds(pl.multiple_of(g * row_count, row_count), row_count)

    def take(g):
        rows = span(g)
        x = jnp.concatenate([gath[g, h, :part_rows, :] for h in range(2)], axis=0)
        cells[rows, :] = x
        ids = gath[g, 0, part_rows:, :][:1, :].astype(f32).astype(jnp.int32)
        attach[:, rows] = onehot(ids, nodes).astype(b16)
        pre = dot(x, enc[...])
        pre_s[...] = pre
        hid_s[rows, :] = (pre * jax.nn.sigmoid(pre)).astype(b16)
        own = pre_s[:, mine]
        sig = jax.nn.sigmoid(own)
        slope_s[rows, :] = sig * (1.0 + own * (1.0 - sig))

    locals_[0].wait()
    weights[0].wait_recv()
    passes = []
    take(me)
    for d in range(1, groups):
        sends[d - 1].wait_recv()
        passes.append(hand_on(gath, d, pass_send, pass_recv))
        if d > 1:
            passes[d - 2].wait_recv()
            take((me - d + 1 + groups) % groups)
    passes[groups - 2].wait_recv()
    take((me + 1) % groups)

    node_in = dot(attach[...], hid_s[...]).astype(b16)
    owned = gath[0, 0, part_rows:, :].astype(f32)
    linked = gath[0, 1, part_rows:, :].astype(f32)
    for g in range(1, groups):
        owned = owned + gath[g, 0, part_rows:, :].astype(f32)
        linked = linked + gath[g, 1, part_rows:, :].astype(f32)
    owned = jnp.concatenate([owned[:IDS], owned[IDS:]], axis=1)
    linked = jnp.concatenate([linked[:IDS], linked[IDS:]], axis=1)[:, :nodes].astype(jnp.int32)
    edges = onehot(linked[0:1], nodes)
    for k in range(1, IDS):
        edges = edges + onehot(linked[k : k + 1], nodes)
    edges = edges.astype(b16)
    to_coarse = onehot(owned[1:2, :nodes].astype(jnp.int32), coarse_count).astype(b16)

    cot_passes = []
    for d in range(1, groups):
        cot_sends[d - 1].wait_recv()
        cot_passes.append(hand_on(gath_cot, d, cot_pass_send, cot_pass_recv))

    agg = row_dot(edges, node_in).astype(b16)
    agg_out[...] = agg
    locals_[2].wait()
    weights[2].wait_recv()
    pre_mesh = dot(agg, proc[...])
    sig_mesh = jax.nn.sigmoid(pre_mesh)
    level_one = node_in.astype(f32) + pre_mesh * sig_mesh
    upper = level_one.astype(b16)
    lower = (level_one - upper.astype(f32)).astype(b16)
    coarse_in = (dot(to_coarse, upper) + dot(to_coarse, lower)).astype(b16)
    locals_[3].wait()
    weights[3].wait_recv()
    pre_coarse = dot(coarse_in, coarse[...])
    sig_coarse = jax.nn.sigmoid(pre_coarse)
    coarse_out = (pre_coarse * sig_coarse).astype(b16)
    level_two = (level_one + row_dot(to_coarse, coarse_out)).astype(b16)
    two_s[...] = level_two

    own_rows = span(me)
    locals_[1].wait()
    weights[1].wait_recv()
    for copy in cot_passes:
        copy.wait_recv()
    cot[...] = gath_cot[...].reshape(cot.shape)
    node_cot = dot(attach[...], cot[...]).astype(b16)
    merged = (
        hid_s[own_rows, :].astype(f32) + row_dot(attach[:, own_rows], level_two)
    ).astype(b16)
    prediction[...] = dot(merged, dec[...])
    decode_grad[...] = row_dot(hid_s[:, mine], cot[...]) + row_dot(two_s[:, mine], node_cot)

    grad_two = col_dot(node_cot, dec[...])
    coarse_cot = dot(to_coarse, node_cot).astype(b16)
    grad_coarse_out = col_dot(coarse_cot, dec[...])
    grad_pre_coarse = grad_coarse_out * (
        sig_coarse * (1.0 + pre_coarse * (1.0 - sig_coarse))
    )
    gpc = grad_pre_coarse.astype(b16)
    gpc_s[...] = gpc
    coarse_in_out[...] = coarse_in
    gpc_out[...] = gpc_s[:, mine]
    grad_coarse_in = col_dot(gpc, coarse[...]).astype(b16)
    grad_one = grad_two + row_dot(to_coarse, grad_coarse_in)
    one_s[...] = grad_one
    gpm = (grad_one * (sig_mesh * (1.0 + pre_mesh * (1.0 - sig_mesh)))).astype(b16)
    gpm_s[...] = gpm
    gpm_out[...] = gpm_s[:, mine]
    grad_agg = col_dot(gpm, proc[mine, :]).astype(b16)
    grad_zero = (one_s[:, mine] + dot(edges, grad_agg)).astype(b16)
    grad_hidden = col_dot(cot[...], dec[mine, :]) + row_dot(attach[...], grad_zero)
    grad_pre = (grad_hidden * slope_s[...]).astype(b16)
    encode_grad[...] = row_dot(cells[...], grad_pre)

    for copy in sends + passes + cot_sends + cot_passes + weights:
        copy.wait_send()


def product_kernel(
    pred_in, encode_in, decode_in, agg, gpm, coarse_in, gpc,
    prediction, encode_grad, process_grad, coarse_grad, decode_grad,
):
    prediction[...] = pred_in[...]
    encode_grad[...] = encode_in[...]
    decode_grad[...] = decode_in[...]
    process_grad[...] = row_dot(agg[...], gpm[...])
    coarse_grad[...] = row_dot(coarse_in[...], gpc[...])


def replicated_body(
    fields, owner_group, owner_node, stencil_codes, coarse_ids,
    encode_weight, process_weight, coarse_weight, decode_weight, cotangent,
):
    f32, b16 = jnp.float32, jnp.bfloat16
    mesh_count, tile_count = lax.axis_size("mesh"), lax.axis_size("tile")
    groups = mesh_count * tile_count
    nodes = MA * MB * groups
    row_count, c_in = fields.shape
    c_out = cotangent.shape[1]
    half = encode_weight.shape[1]
    full = process_weight.shape[0]
    coarse_count = CPD * groups
    total_rows = row_count * groups
    any_spec = pl.BlockSpec(memory_space=pl.ANY)
    vmem = pl.BlockSpec(memory_space=pltpu.VMEM)
    shape = lambda *dims: jax.ShapeDtypeStruct(dims, f32)
    short = lambda *dims: jax.ShapeDtypeStruct(dims, b16)
    part_rows = row_count // 2
    parts = pl.pallas_call(
        functools.partial(step_kernel, mesh_count, tile_count),
        out_shape=[
            shape(row_count, c_out), shape(c_in, half), shape(half, c_out),
            short(nodes, full), short(nodes, half), short(coarse_count, full),
            short(coarse_count, half),
        ],
        in_specs=[vmem] * 6 + [any_spec] * 4,
        out_specs=[vmem] * 7,
        scratch_shapes=[
            pltpu.VMEM((groups, 2, part_rows + 2 * IDS, c_in), b16),
            pltpu.VMEM((groups, 2, part_rows, c_out), b16),
            pltpu.VMEM((c_in, full), b16),
            pltpu.VMEM((full, full), b16),
            pltpu.VMEM((full, full), b16),
            pltpu.VMEM((full, c_out), b16),
            pltpu.VMEM((total_rows, c_in), b16),
            pltpu.VMEM((total_rows, c_out), b16),
            pltpu.VMEM((nodes, total_rows), b16),
            pltpu.VMEM((row_count, full), f32),
            pltpu.VMEM((total_rows, full), b16),
            pltpu.VMEM((total_rows, half), f32),
            pltpu.VMEM((nodes, full), f32),
            pltpu.VMEM((nodes, full), b16),
            pltpu.VMEM((nodes, full), b16),
            pltpu.VMEM((coarse_count, full), b16),
        ]
        + [pltpu.SemaphoreType.DMA((groups,))] * 8
        + [pltpu.SemaphoreType.DMA((4,))] * 3,
        compiler_params=pltpu.CompilerParams(collective_id=0, has_side_effects=True),
        name="step",
    )(
        fields, owner_group.reshape(1, -1), owner_node.reshape(1, -1),
        stencil_codes.T, coarse_ids.reshape(1, -1), cotangent,
        encode_weight, process_weight, coarse_weight, decode_weight,
    )
    return tuple(
        pl.pallas_call(
            product_kernel,
            out_shape=[
                shape(row_count, c_out), shape(c_in, half), shape(full, half),
                shape(full, half), shape(half, c_out),
            ],
            in_specs=[vmem] * 7,
            out_specs=[vmem] * 5,
            name="products",
        )(*parts)
    )


def any_size(*args):
    groups = lax.axis_size("mesh") * lax.axis_size("tile")
    row_count, c_in = args[0].shape
    nodes = MA * MB * groups
    aligned = row_count % 128 == 0 and c_in == row_count and args[3].shape[1] == IDS
    fits = nodes <= min(256, 2 * row_count) and aligned and lax.axis_size("feat") == 2
    return (replicated_body if fits else body)(*args)


def solution(mesh):
    placed = (
        P(("parts", "mesh", "tile"), None),
        P(("mesh", "tile"), None),
        P(("mesh", "tile")),
        P(("mesh", "tile"), None),
        P(("mesh", "tile")),
        P(None, "feat"),
        P(None, "feat"),
        P(None, "feat"),
        P("feat", None),
        P(("parts", "mesh", "tile"), None),
    )
    return jax.shard_map(
        any_size,
        mesh=mesh,
        in_specs=placed,
        out_specs=(
            P(("parts", "mesh", "tile"), None),
            P("parts", "feat"),
            P("parts", "feat"),
            P("parts", "feat"),
            P(("parts", "feat"), None),
        ),
        check_vma=False,
    )
```

```python
import functools

import jax
import jax.numpy as jnp
from jax import lax
from jax.experimental import pallas as pl
from jax.experimental.pallas import tpu as pltpu
from jax.sharding import PartitionSpec as P

MA = 4
MB = 8
CPD = 2


def padded(array, sides, width):
    for axis, dim in sides:
        peers, length = (lax.axis_size(axis), array.shape[dim])
        up = [(i, (i + 1) % peers) for i in range(peers)]
        down = [(j, i) for i, j in up]
        last = lax.slice_in_dim(array, length - width, length, axis=dim)
        initial = lax.slice_in_dim(array, 0, width, axis=dim)
        before = lax.ppermute(last, axis, up)
        after = lax.ppermute(initial, axis, down)
        array = jnp.concatenate([before, array, after], axis=dim)
    return array


def silu_grad(pre):
    sig = jax.nn.sigmoid(pre)
    return sig * (1.0 + pre * (1.0 - sig))


def send_rows(outgoing, slot_node):
    feat_width = outgoing.shape[-1]
    got, got_node = (
        lax.all_to_all(outgoing, ("mesh", "tile"), split_axis=0, concat_axis=0, tiled=True),
        lax.all_to_all(slot_node, ("mesh", "tile"), split_axis=0, concat_axis=0, tiled=True),
    )
    return (got.reshape(-1, feat_width), got_node.reshape(-1))


def route_block(block, mesh_count, tile_count, purpose):
    feat_width = block.shape[-1]
    slot_count = block.shape[0] // (mesh_count * tile_count)
    flat_shape = (mesh_count * tile_count, slot_count, feat_width)
    if purpose == "reply":
        moved = lax.all_to_all(
            block.reshape(flat_shape), ("mesh", "tile"), split_axis=0, concat_axis=0, tiled=True
        )
    elif purpose == "gradient":
        moved = lax.all_to_all(
            block.reshape(flat_shape), ("mesh", "tile"), split_axis=0, concat_axis=0, tiled=True
        )
    else:
        moved = lax.all_to_all(
            block.reshape(flat_shape), ("mesh", "tile"), split_axis=0, concat_axis=0, tiled=True
        )
    return moved.reshape(-1, feat_width)


def body(
    fields,
    owner_group,
    owner_node,
    stencil_codes,
    coarse_ids,
    encode_weight,
    process_weight,
    coarse_weight,
    decode_weight,
    cotangent,
):
    highest = lax.Precision.HIGHEST
    row_count = fields.shape[0]
    mesh_count = lax.axis_size("mesh")
    tile_count = lax.axis_size("tile")
    groups = mesh_count * tile_count
    slot_count = 2 * row_count // groups
    feat_width = encode_weight.shape[1]
    patch_rows = MA
    patch_cols = MB
    nodes_local = patch_rows * patch_cols
    coarse_count = CPD * groups
    target = owner_group[:, 0]
    group_onehot = (target[:, None] == jnp.arange(groups, dtype=jnp.int32)[None, :]).astype(
        jnp.int32
    )
    earlier = jnp.cumsum(group_onehot, axis=0) - group_onehot
    position = target * slot_count + jnp.sum(earlier * group_onehot, axis=1)
    matches = jnp.arange(groups * slot_count, dtype=jnp.int32)[:, None] == position[None, :]
    dispatch = matches.astype(jnp.bfloat16)
    slot_node = (jnp.max(jnp.where(matches, owner_node[None, :] + 1, 0), axis=1) - 1).reshape(
        groups, slot_count
    )
    pre_encode = jnp.dot(fields, encode_weight, preferred_element_type=jnp.float32)
    hidden = jax.nn.silu(pre_encode).astype(jnp.bfloat16)
    outgoing = jnp.dot(dispatch, hidden, preferred_element_type=jnp.float32).astype(jnp.bfloat16)
    incoming, incoming_node = send_rows(outgoing.reshape(groups, slot_count, feat_width), slot_node)
    node_match = (
        incoming_node[:, None] == jnp.arange(nodes_local, dtype=jnp.int32)[None, :]
    ).astype(jnp.bfloat16)
    node_in = jnp.einsum(
        "sn,sh->nh", node_match, incoming, preferred_element_type=jnp.float32
    ).astype(jnp.bfloat16)
    counts = jnp.sum(
        (stencil_codes[:, :, None] == jnp.arange(25, dtype=jnp.int32)[None, None, :]).astype(
            jnp.float32
        ),
        axis=1,
    )
    counts = counts.astype(jnp.bfloat16).reshape(patch_rows, patch_cols, 25)
    padded_nodes, padded_counts = (
        padded(node_in.reshape(patch_rows, patch_cols, feat_width), (("mesh", 0), ("tile", 1)), 2),
        padded(counts, (("mesh", 0), ("tile", 1)), 2),
    )
    gathered = jnp.zeros((patch_rows, patch_cols, feat_width), jnp.float32)
    for code_index in range(25):
        step_x = code_index // 5 - 2
        step_y = code_index % 5 - 2
        weight_here = padded_counts[
            2 : 2 + patch_rows, 2 : 2 + patch_cols, code_index : code_index + 1
        ].astype(jnp.float32)
        gathered = gathered + weight_here * padded_nodes[
            2 + step_x : 2 + step_x + patch_rows, 2 + step_y : 2 + step_y + patch_cols
        ].astype(jnp.float32)
    agg = gathered.reshape(nodes_local, feat_width).astype(jnp.bfloat16)
    agg_full = lax.all_gather(agg, "feat", axis=1, tiled=True)
    pre_mesh = jnp.dot(agg_full, process_weight, preferred_element_type=jnp.float32)
    level_one = node_in.astype(jnp.float32) + jax.nn.silu(pre_mesh)
    coarse_match = (
        coarse_ids[:, None] == jnp.arange(coarse_count, dtype=jnp.int32)[None, :]
    ).astype(jnp.float32)
    coarse_part = jnp.dot(coarse_match.T, level_one, precision=highest)
    coarse_total = lax.psum(coarse_part, ("mesh", "tile"))
    coarse_in = lax.all_gather(coarse_total.astype(jnp.bfloat16), "feat", axis=1, tiled=True)
    pre_coarse = jnp.dot(coarse_in, coarse_weight, preferred_element_type=jnp.float32)
    coarse_out = jax.nn.silu(pre_coarse).astype(jnp.bfloat16)
    level_two = (
        level_one
        + jnp.dot(coarse_match.astype(jnp.bfloat16), coarse_out, preferred_element_type=jnp.float32)
    ).astype(jnp.bfloat16)
    reply_rows = jnp.dot(node_match, level_two, preferred_element_type=jnp.float32).astype(
        jnp.bfloat16
    )
    returned = route_block(reply_rows, mesh_count, tile_count, "reply")
    merged = (
        hidden.astype(jnp.float32)
        + jnp.einsum("sr,sh->rh", dispatch, returned, preferred_element_type=jnp.float32)
    ).astype(jnp.bfloat16)
    pred_part = jnp.dot(merged, decode_weight, preferred_element_type=jnp.float32)
    prediction = lax.psum(pred_part, "feat")
    decode_grad = jnp.dot(merged.astype(jnp.float32).T, cotangent, precision=highest)
    grad_merged = jnp.dot(cotangent, decode_weight.astype(jnp.float32).T, precision=highest)
    grad_out = jnp.dot(
        dispatch, grad_merged.astype(jnp.bfloat16), preferred_element_type=jnp.float32
    ).astype(jnp.bfloat16)
    grad_in = route_block(grad_out, mesh_count, tile_count, "gradient")
    grad_two = jnp.einsum("sn,sh->nh", node_match, grad_in, preferred_element_type=jnp.float32)
    coarse_grad_part = jnp.dot(coarse_match.T, grad_two, precision=highest)
    grad_coarse_out = lax.psum(coarse_grad_part, ("mesh", "tile"))
    grad_pre_coarse = grad_coarse_out * silu_grad(pre_coarse)
    coarse_grad = jnp.dot(coarse_in.astype(jnp.float32).T, grad_pre_coarse, precision=highest)
    grad_coarse_full = jnp.dot(
        grad_pre_coarse, coarse_weight.astype(jnp.float32).T, precision=highest
    )
    grad_coarse_in = lax.psum_scatter(grad_coarse_full, "feat", scatter_dimension=1, tiled=True)
    grad_one = grad_two + jnp.dot(coarse_match, grad_coarse_in, precision=highest)
    grad_pre_mesh = grad_one * silu_grad(pre_mesh)
    process_grad = jnp.dot(agg_full.astype(jnp.float32).T, grad_pre_mesh, precision=highest)
    grad_pre_full = lax.all_gather(grad_pre_mesh, "feat", axis=1, tiled=True)
    weight_full = lax.all_gather(process_weight, "feat", axis=1, tiled=True)
    own_rows = lax.dynamic_slice_in_dim(
        weight_full, lax.axis_index("feat") * feat_width, feat_width, 0
    )
    grad_agg = jnp.dot(grad_pre_full, own_rows.astype(jnp.float32).T, precision=highest).astype(
        jnp.bfloat16
    )
    padded_grad = padded(
        grad_agg.reshape(patch_rows, patch_cols, feat_width), (("mesh", 0), ("tile", 1)), 2
    )
    spread = jnp.zeros((patch_rows, patch_cols, feat_width), jnp.float32)
    for code_index in range(25):
        step_x = code_index // 5 - 2
        step_y = code_index % 5 - 2
        weight_there = padded_counts[
            2 - step_x : 2 - step_x + patch_rows,
            2 - step_y : 2 - step_y + patch_cols,
            code_index : code_index + 1,
        ].astype(jnp.float32)
        spread = spread + weight_there * padded_grad[
            2 - step_x : 2 - step_x + patch_rows, 2 - step_y : 2 - step_y + patch_cols
        ].astype(jnp.float32)
    grad_zero = (grad_one + spread.reshape(nodes_local, feat_width)).astype(jnp.bfloat16)
    back_rows = jnp.dot(node_match, grad_zero, preferred_element_type=jnp.float32).astype(
        jnp.bfloat16
    )
    grad_back = route_block(back_rows, mesh_count, tile_count, "return")
    grad_hidden = grad_merged + jnp.einsum(
        "sr,sh->rh", dispatch, grad_back, preferred_element_type=jnp.float32
    )
    grad_pre_encode = grad_hidden * silu_grad(pre_encode)
    encode_grad = jnp.dot(fields.astype(jnp.float32).T, grad_pre_encode, precision=highest)
    encode_grad, process_grad, decode_grad = lax.psum(
        (encode_grad, process_grad, decode_grad), ("mesh", "tile")
    )
    return (prediction, encode_grad, process_grad, coarse_grad, decode_grad)


MESH = pl.DeviceIdType.MESH
ROW_DIMS = (((0,), (0,)), ((), ()))
COL_DIMS = (((1,), (1,)), ((), ()))
IDS = 8


def quotient(values, divisor):
    return jnp.floor((values.astype(jnp.float32) + 0.5) * (1.0 / divisor)).astype(jnp.int32)


def onehot(ids, count):
    numbers = lax.broadcasted_iota(jnp.int32, (count, ids.shape[1]), 0)
    return jnp.where(numbers == ids, 1.0, 0.0)


def dot(a, b):
    return jnp.dot(a, b, preferred_element_type=jnp.float32)


def row_dot(a, b):
    return lax.dot_general(a, b, ROW_DIMS, preferred_element_type=jnp.float32)


def col_dot(a, b):
    return lax.dot_general(a, b, COL_DIMS, preferred_element_type=jnp.float32)


def step_kernel(
    mesh_count, tile_count,
    fields_in, owner_group_in, owner_node_in, codes_in, coarse_ids_in, cotangent_in,
    enc_n, proc_n, coarse_n, dec_n,
    prediction, encode_grad, decode_grad, agg_out, gpm_out, coarse_in_out, gpc_out,
    gath, gath_cot, enc, proc, coarse, dec, cells, cot, attach, pre_s, hid_s, slope_s, one_s, two_s, gpm_s, gpc_s,
    send_sem, recv_sem, pass_send, pass_recv, cot_send, cot_recv, cot_pass_send, cot_pass_recv,
    weight_send, weight_recv, local_sem,
    fields, owner_group, owner_node, codes, coarse_ids, cotangent, input_sem,
):
    f32, b16 = jnp.float32, jnp.bfloat16
    groups = mesh_count * tile_count
    m, t, feat = lax.axis_index("mesh"), lax.axis_index("tile"), lax.axis_index("feat")
    me = m * tile_count + t
    sibling = {"feat": 1 - feat}
    nodes_local = MA * MB
    nodes = nodes_local * groups
    coarse_count = CPD * groups
    row_count, c_in = fields.shape
    width = 2 * row_count
    part_rows = row_count // 2
    half = enc_n.shape[1]
    mine = pl.ds(pl.multiple_of(feat * half, half), half)

    def place(group):
        return {"mesh": group // tile_count, "tile": group % tile_count}

    barrier = pltpu.get_barrier_semaphore()
    pl.semaphore_signal(barrier, inc=1, device_id=sibling, device_id_type=MESH)
    for d in range(1, groups):
        pl.semaphore_signal(
            barrier, inc=1, device_id=place((me + d) % groups), device_id_type=MESH
        )

    pairs = (
        (enc_n, enc.at[:, mine]), (dec_n, dec.at[mine, :]),
        (proc_n, proc.at[:, mine]), (coarse_n, coarse.at[:, mine]),
    )
    inputs = (
        (codes_in, codes), (coarse_ids_in, coarse_ids), (owner_group_in, owner_group),
        (owner_node_in, owner_node), (fields_in, fields), (cotangent_in, cotangent),
    )
    loads = []
    for i, (src, dst) in enumerate(inputs):
        copy = pltpu.make_async_copy(src, dst, input_sem.at[i])
        copy.start()
        loads.append(copy)
    locals_ = []
    for i, (src, dst) in enumerate(pairs):
        copy = pltpu.make_async_copy(src, dst, local_sem.at[i])
        copy.start()
        locals_.append(copy)

    for copy in loads:
        copy.wait()
    own_cot = cotangent[...].astype(b16)
    for h in range(2):
        gath[me, h, :part_rows, :] = fields[h * part_rows : (h + 1) * part_rows, :]
        gath_cot[me, h] = own_cot[h * part_rows : (h + 1) * part_rows]
    code = codes[...]
    code_row = sum(jnp.where(code >= 5 * i, 1, 0) for i in range(1, 5))
    local = lax.broadcasted_iota(jnp.int32, (1, nodes_local), 1)
    local_row = quotient(local, MB)
    row = m * MA + local_row + code_row - 2
    col = t * MB + (local - local_row * MB) + (code - 5 * code_row) - 2
    rows_all, cols_all = mesh_count * MA, tile_count * MB
    for _ in range(2):
        row = jnp.where(row < 0, row + rows_all, jnp.where(row >= rows_all, row - rows_all, row))
        col = jnp.where(col < 0, col + cols_all, jnp.where(col >= cols_all, col - cols_all, col))
    row_group, col_group = quotient(row, MA), quotient(col, MB)
    near = (
        (row_group * tile_count + col_group) * nodes_local
        + (row - row_group * MA) * MB + col - col_group * MB
    )
    spot = jnp.where(
        lax.broadcasted_iota(jnp.int32, (nodes_local, width), 1)
        == lax.broadcasted_iota(jnp.int32, (nodes_local, width), 0) + nodes_local * me,
        1.0, 0.0,
    ).astype(b16)
    order = lax.broadcasted_iota(jnp.int32, (IDS, nodes_local), 0)
    owned = jnp.where(order == 1, coarse_ids[...], 0).astype(f32).astype(b16)
    owned = dot(owned, spot)
    target = (owner_group[...] * nodes_local + owner_node[...]).astype(f32)
    order = lax.broadcasted_iota(jnp.int32, (IDS, row_count), 0)
    named = jnp.where(order == 0, target, owned[:, :row_count])
    linked = dot(near.astype(f32).astype(b16), spot)
    gath[me, 0, part_rows:, :] = jnp.concatenate([named, owned[:, row_count:]], axis=0).astype(b16)
    gath[me, 1, part_rows:, :] = jnp.concatenate(
        [linked[:, :row_count], linked[:, row_count:]], axis=0
    ).astype(b16)

    pl.semaphore_wait(barrier, groups)

    def spread(buffer, send, recv):
        copies = []
        for d in range(1, groups):
            copy = pltpu.make_async_remote_copy(
                src_ref=buffer.at[me, feat], dst_ref=buffer.at[me, feat],
                send_sem=send.at[d], recv_sem=recv.at[d],
                device_id=place((me + d) % groups), device_id_type=MESH,
            )
            copy.start()
            copies.append(copy)
        return copies

    def hand_on(buffer, d, send, recv):
        came = (me - d + groups) % groups
        copy = pltpu.make_async_remote_copy(
            src_ref=buffer.at[came, feat], dst_ref=buffer.at[came, feat],
            send_sem=send.at[d], recv_sem=recv.at[d],
            device_id=sibling, device_id_type=MESH,
        )
        copy.start()
        return copy

    sends = spread(gath, send_sem, recv_sem)
    cot_sends = spread(gath_cot, cot_send, cot_recv)
    weights = []
    for i, (src, dst) in enumerate(pairs):
        copy = pltpu.make_async_remote_copy(
            src_ref=src, dst_ref=dst,
            send_sem=weight_send.at[i], recv_sem=weight_recv.at[i],
            device_id=sibling, device_id_type=MESH,
        )
        copy.start()
        weights.append(copy)

    def span(g):
        return pl.ds(pl.multiple_of(g * row_count, row_count), row_count)

    def take(g):
        rows = span(g)
        x = jnp.concatenate([gath[g, h, :part_rows, :] for h in range(2)], axis=0)
        cells[rows, :] = x
        ids = gath[g, 0, part_rows:, :][:1, :].astype(f32).astype(jnp.int32)
        attach[:, rows] = onehot(ids, nodes).astype(b16)
        pre = dot(x, enc[...])
        pre_s[...] = pre
        hid_s[rows, :] = (pre * jax.nn.sigmoid(pre)).astype(b16)
        own = pre_s[:, mine]
        sig = jax.nn.sigmoid(own)
        slope_s[rows, :] = sig * (1.0 + own * (1.0 - sig))

    locals_[0].wait()
    weights[0].wait_recv()
    passes = []
    take(me)
    for d in range(1, groups):
        sends[d - 1].wait_recv()
        passes.append(hand_on(gath, d, pass_send, pass_recv))
        if d > 1:
            passes[d - 2].wait_recv()
            take((me - d + 1 + groups) % groups)
    passes[groups - 2].wait_recv()
    take((me + 1) % groups)

    cot_passes = []
    for d in range(1, groups):
        cot_sends[d - 1].wait_recv()
        cot_passes.append(hand_on(gath_cot, d, cot_pass_send, cot_pass_recv))
    node_in = dot(attach[...], hid_s[...]).astype(b16)
    owned = gath[0, 0, part_rows:, :].astype(f32)
    linked = gath[0, 1, part_rows:, :].astype(f32)
    for g in range(1, groups):
        owned = owned + gath[g, 0, part_rows:, :].astype(f32)
        linked = linked + gath[g, 1, part_rows:, :].astype(f32)
    owned = jnp.concatenate([owned[:IDS], owned[IDS:]], axis=1)
    linked = jnp.concatenate([linked[:IDS], linked[IDS:]], axis=1)[:, :nodes].astype(jnp.int32)
    edges = onehot(linked[0:1], nodes)
    for k in range(1, IDS):
        edges = edges + onehot(linked[k : k + 1], nodes)
    edges = edges.astype(b16)
    to_coarse = onehot(owned[1:2, :nodes].astype(jnp.int32), coarse_count).astype(b16)

    agg = row_dot(edges, node_in).astype(b16)
    agg_out[...] = agg
    locals_[2].wait()
    weights[2].wait_recv()
    pre_mesh = dot(agg, proc[...])
    sig_mesh = jax.nn.sigmoid(pre_mesh)
    level_one = node_in.astype(f32) + pre_mesh * sig_mesh
    upper = level_one.astype(b16)
    lower = (level_one - upper.astype(f32)).astype(b16)
    coarse_in = (dot(to_coarse, upper) + dot(to_coarse, lower)).astype(b16)
    locals_[3].wait()
    weights[3].wait_recv()
    pre_coarse = dot(coarse_in, coarse[...])
    sig_coarse = jax.nn.sigmoid(pre_coarse)
    coarse_out = (pre_coarse * sig_coarse).astype(b16)
    level_two = (level_one + row_dot(to_coarse, coarse_out)).astype(b16)
    two_s[...] = level_two

    own_rows = span(me)
    locals_[1].wait()
    weights[1].wait_recv()
    for copy in cot_passes:
        copy.wait_recv()
    cot[...] = gath_cot[...].reshape(cot.shape)
    node_cot = dot(attach[...], cot[...]).astype(b16)
    merged = (
        hid_s[own_rows, :].astype(f32) + row_dot(attach[:, own_rows], level_two)
    ).astype(b16)
    prediction[...] = dot(merged, dec[...])
    decode_grad[...] = row_dot(hid_s[:, mine], cot[...]) + row_dot(two_s[:, mine], node_cot)

    grad_two = col_dot(node_cot, dec[...])
    coarse_cot = dot(to_coarse, node_cot).astype(b16)
    grad_coarse_out = col_dot(coarse_cot, dec[...])
    grad_pre_coarse = grad_coarse_out * (
        sig_coarse * (1.0 + pre_coarse * (1.0 - sig_coarse))
    )
    gpc = grad_pre_coarse.astype(b16)
    gpc_s[...] = gpc
    coarse_in_out[...] = coarse_in
    gpc_out[...] = gpc_s[:, mine]
    grad_coarse_in = col_dot(gpc, coarse[...]).astype(b16)
    grad_one = grad_two + row_dot(to_coarse, grad_coarse_in)
    one_s[...] = grad_one
    gpm = (grad_one * (sig_mesh * (1.0 + pre_mesh * (1.0 - sig_mesh)))).astype(b16)
    gpm_s[...] = gpm
    gpm_out[...] = gpm_s[:, mine]
    grad_agg = col_dot(gpm, proc[mine, :]).astype(b16)
    grad_zero = (one_s[:, mine] + dot(edges, grad_agg)).astype(b16)
    grad_hidden = col_dot(cot[...], dec[mine, :]) + row_dot(attach[...], grad_zero)
    grad_pre = (grad_hidden * slope_s[...]).astype(b16)
    encode_grad[...] = row_dot(cells[...], grad_pre)

    for copy in sends + passes + cot_sends + cot_passes + weights:
        copy.wait_send()


def product_kernel(
    pred_in, encode_in, decode_in, agg, gpm, coarse_in, gpc,
    prediction, encode_grad, process_grad, coarse_grad, decode_grad,
):
    prediction[...] = pred_in[...]
    encode_grad[...] = encode_in[...]
    decode_grad[...] = decode_in[...]
    process_grad[...] = row_dot(agg[...], gpm[...])
    coarse_grad[...] = row_dot(coarse_in[...], gpc[...])


def replicated_body(
    fields, owner_group, owner_node, stencil_codes, coarse_ids,
    encode_weight, process_weight, coarse_weight, decode_weight, cotangent,
):
    f32, b16 = jnp.float32, jnp.bfloat16
    mesh_count, tile_count = lax.axis_size("mesh"), lax.axis_size("tile")
    groups = mesh_count * tile_count
    nodes = MA * MB * groups
    row_count, c_in = fields.shape
    c_out = cotangent.shape[1]
    half = encode_weight.shape[1]
    full = process_weight.shape[0]
    coarse_count = CPD * groups
    total_rows = row_count * groups
    any_spec = pl.BlockSpec(memory_space=pl.ANY)
    vmem = pl.BlockSpec(memory_space=pltpu.VMEM)
    shape = lambda *dims: jax.ShapeDtypeStruct(dims, f32)
    part_rows = row_count // 2
    parts = pl.pallas_call(
        functools.partial(step_kernel, mesh_count, tile_count),
        out_shape=[
            pltpu.VMEM((row_count, c_out), f32), pltpu.VMEM((c_in, half), f32),
            pltpu.VMEM((half, c_out), f32), pltpu.VMEM((nodes, full), b16),
            pltpu.VMEM((nodes, half), b16), pltpu.VMEM((coarse_count, full), b16),
            pltpu.VMEM((coarse_count, half), b16),
        ],
        in_specs=[any_spec] * 10,
        out_specs=[vmem] * 7,
        scratch_shapes=[
            pltpu.VMEM((groups, 2, part_rows + 2 * IDS, c_in), b16),
            pltpu.VMEM((groups, 2, part_rows, c_out), b16),
            pltpu.VMEM((c_in, full), b16),
            pltpu.VMEM((full, full), b16),
            pltpu.VMEM((full, full), b16),
            pltpu.VMEM((full, c_out), b16),
            pltpu.VMEM((total_rows, c_in), b16),
            pltpu.VMEM((total_rows, c_out), b16),
            pltpu.VMEM((nodes, total_rows), b16),
            pltpu.VMEM((row_count, full), f32),
            pltpu.VMEM((total_rows, full), b16),
            pltpu.VMEM((total_rows, half), f32),
            pltpu.VMEM((nodes, full), f32),
            pltpu.VMEM((nodes, full), b16),
            pltpu.VMEM((nodes, full), b16),
            pltpu.VMEM((coarse_count, full), b16),
        ]
        + [pltpu.SemaphoreType.DMA((groups,))] * 8
        + [pltpu.SemaphoreType.DMA((4,))] * 3
        + [
            pltpu.VMEM((row_count, c_in), b16),
            pltpu.VMEM((1, row_count), jnp.int32),
            pltpu.VMEM((1, row_count), jnp.int32),
            pltpu.VMEM((IDS, MA * MB), jnp.int32),
            pltpu.VMEM((1, MA * MB), jnp.int32),
            pltpu.VMEM((row_count, c_out), f32),
            pltpu.SemaphoreType.DMA((6,)),
        ],
        compiler_params=pltpu.CompilerParams(collective_id=0, has_side_effects=True),
        name="step",
    )(
        fields, owner_group.reshape(1, -1), owner_node.reshape(1, -1),
        stencil_codes.T, coarse_ids.reshape(1, -1), cotangent,
        encode_weight, process_weight, coarse_weight, decode_weight,
    )
    return tuple(
        pl.pallas_call(
            product_kernel,
            out_shape=[
                shape(row_count, c_out), shape(c_in, half), shape(full, half),
                shape(full, half), shape(half, c_out),
            ],
            in_specs=[vmem] * 7,
            out_specs=[vmem] * 5,
            compiler_params=pltpu.CompilerParams(vmem_limit_bytes=32 * 2**20),
            name="products",
        )(*parts)
    )


def any_size(*args):
    groups = lax.axis_size("mesh") * lax.axis_size("tile")
    row_count, c_in = args[0].shape
    nodes = MA * MB * groups
    aligned = row_count % 128 == 0 and c_in == row_count and args[3].shape[1] == IDS
    fits = nodes <= min(256, 2 * row_count) and aligned and lax.axis_size("feat") == 2
    return (replicated_body if fits else body)(*args)


def solution(mesh):
    placed = (
        P(("parts", "mesh", "tile"), None),
        P(("mesh", "tile"), None),
        P(("mesh", "tile")),
        P(("mesh", "tile"), None),
        P(("mesh", "tile")),
        P(None, "feat"),
        P(None, "feat"),
        P(None, "feat"),
        P("feat", None),
        P(("parts", "mesh", "tile"), None),
    )
    return jax.shard_map(
        any_size,
        mesh=mesh,
        in_specs=placed,
        out_specs=(
            P(("parts", "mesh", "tile"), None),
            P("parts", "feat"),
            P("parts", "feat"),
            P("parts", "feat"),
            P(("parts", "feat"), None),
        ),
        check_vma=False,
    )
```
